256 devices in a mesh: dp: 64 (over z, x, y_hi), tensor: 4 (over y_lo, core).
Axes of the slice: x: 4, y: 4 (y_hi: 2, y_lo: 2; y = y_hi * 2 + y_lo), z: 8, core: 2. Of those that a mesh axis runs over, the one named last changes fastest.
Arguments:
- d_out: bfloat16 [16384, 3072], P('dp'), may hold values from -12 to 12
- gate: bfloat16 [16384, 4096], P('dp', 'tensor'), may hold values from -16 to 16
- up_proj: bfloat16 [16384, 4096], P('dp', 'tensor'), may hold values from -12 to 12
- master: float32 [4096, 3072], P(('tensor', 'dp')), may hold values from -0.09375 to 0.09375
- moment_one: float32 [4096, 3072], P(('tensor', 'dp')), may hold values from -4 to 4
- moment_two: float32 [4096, 3072], P(('tensor', 'dp')), may hold values from 0.05 to 2
Outputs:
- gate_grad: bfloat16 [16384, 4096], P('dp', 'tensor')
- up_grad: bfloat16 [16384, 4096], P('dp', 'tensor')
- master_next: float32 [4096, 3072], P(('tensor', 'dp'))
- moment_one_next: float32 [4096, 3072], P(('tensor', 'dp'))
- moment_two_next: float32 [4096, 3072], P(('tensor', 'dp'))
- weight_next: bfloat16 [4096, 3072], P('tensor')
The draws below stay inside these ranges and needn't reach their ends.
All inputs are finite; a program needn't handle non-finite values.
Results may differ from the reference program's by a relative error of at most 0.005.
Values may be sent and summed in bfloat16 or wider, within the bound.
A program may use at most 64 MiB of HBM per device.

```python
import math
import jax
import jax.numpy as jnp

D = 3072
FF = 4096
TOKENS = 16384


def draw_d_out(key, part):
    key_cols, key_base = jax.random.split(key, 2)
    scales = jnp.exp(jax.random.uniform(key_cols, (D,), jnp.float32, jnp.log(0.3), jnp.log(3.0)))
    values = jax.random.normal(key_base, (TOKENS, D), jnp.float32) * scales
    return jnp.clip(values, -12.0, 12.0).astype(jnp.bfloat16)


def draw_up_proj(key, part):
    key_cols, key_base = jax.random.split(key, 2)
    place = jnp.arange(FF, dtype=jnp.float32) / FF
    scales = jnp.exp(jax.random.uniform(key_cols, (FF,), jnp.float32, jnp.log(0.5), jnp.log(1.6)))
    ramp = jnp.sqrt(1.0 + 2.0 * place)
    base = jax.random.normal(key_base, (TOKENS, FF), jnp.float32)
    return jnp.clip(base * scales * ramp, -12.0, 12.0).astype(jnp.bfloat16)


def strengthened(values, key, source, target, parts, factor):
    owner, partner = [(jnp.arange(values.shape[dim]) // (values.shape[dim] // parts)).reshape([-1 if axis == dim else 1 for axis in range(values.ndim)]) for dim in (source, target)]
    chosen = jax.random.permutation(key, parts)[partner]
    strong = (owner == chosen) | (owner == (partner + parts // 2) % parts)
    return jnp.where(strong, factor * values, values)


def levels(rng, dims, pieces, least, largest):
    def one(axis_at, blocks):
        draws = jax.random.uniform(jax.random.fold_in(jax.random.fold_in(rng, 6), axis_at), (blocks,), jnp.float32, least / len(pieces), largest / len(pieces))
        return jnp.repeat(jnp.exp(draws), dims[axis_at] // blocks).reshape((-1,) + (1,) * (len(dims) - axis_at - 1))

    loudness = one(*pieces[0])
    for cut in pieces[1:]:
        loudness = loudness * one(*cut)
    return loudness


def noise(stream_key, dims, deviation, bound, shards=(), kind=jnp.bfloat16):
    loudness = levels(stream_key, dims, shards, -0.22, 0.18) if shards else 1.0
    drawn = jax.random.normal(stream_key, dims, jnp.float32) * deviation * loudness
    return jnp.minimum(jnp.maximum(drawn, -bound), bound).astype(kind)


def bell_draw_with(stream_key, extent, deviation, bound, cuts, heavy, kind=jnp.bfloat16):
    result = deviation * jax.random.normal(stream_key, extent, jnp.float32)
    if cuts:
        result = result * levels(stream_key, extent, cuts, -0.22, 0.18)
    return jnp.clip(strengthened(result, jax.random.fold_in(stream_key, 3), *heavy), -bound, bound).astype(kind)


def setup_inputs(seed: int = 0) -> dict:
    arg_keys = jax.random.split(jax.random.key(seed), 7)
    return {
        "d_out": draw_d_out(jax.random.fold_in(arg_keys[6], 71), 0),
        "gate": bell_draw_with(arg_keys[1], (TOKENS, FF), 1.0, 16.0, ((0, 64), (1, 4)), (0, 1, 64, 4.0)),
        "up_proj": draw_up_proj(jax.random.fold_in(arg_keys[6], 71), 0),
        "master": noise(arg_keys[3], (FF, D), FF ** -0.5, 0.09375, ((0, 256),), jnp.float32),
        "moment_one": noise(arg_keys[4], (FF, D), 0.5, 4.0, ((0, 256),), jnp.float32),
        "moment_two": jnp.clip(jnp.exp(math.log(2.0) - 3.6888794 * jax.random.uniform(arg_keys[5], (FF, D), jnp.float32) ** levels(arg_keys[5], (FF, D), ((0, 256),), -0.2, 0.2)), 0.05, 2.0),
    }


def reference(d_out, gate, up_proj, master, moment_one, moment_two):
    weight = master.astype(jnp.bfloat16)
    gate_f = gate.astype(jnp.float32)
    up_f = up_proj.astype(jnp.float32)
    silu_gate = jax.nn.silu(gate_f)
    hidden = (silu_gate * up_f).astype(jnp.bfloat16)
    d_hidden = jnp.dot(d_out, weight.T, preferred_element_type=jnp.float32)
    up_grad = (d_hidden * silu_gate).astype(jnp.bfloat16)
    sigm = jax.nn.sigmoid(gate_f)
    gate_grad = (d_hidden * up_f * sigm * (1.0 + gate_f * (1.0 - sigm))).astype(jnp.bfloat16)
    grad = jnp.dot(hidden.T, d_out, preferred_element_type=jnp.float32)
    total = jnp.sum(grad * grad)
    factor = 1.0 / jnp.sqrt(total / (FF * D) + 1e-06)
    clipped = grad * factor
    moment_one_next = 0.9 * moment_one + 0.1 * clipped
    moment_two_next = 0.95 * moment_two + 0.05 * clipped * clipped
    master_next = master - 0.003 * (moment_one_next / (jnp.sqrt(moment_two_next) + 1e-08) + 0.1 * master)
    weight_next = master_next.astype(jnp.bfloat16)
    return (gate_grad, up_grad, master_next, moment_one_next, moment_two_next, weight_next)
```

```python
import functools

import jax
import jax.numpy as jnp
from jax import lax
from jax.experimental import pallas as pl
from jax.experimental.pallas import tpu as pltpu
from jax.sharding import PartitionSpec as P

D = 3072
FF = 4096
MESH = pl.DeviceIdType.MESH
F32 = jnp.float32
BF16 = jnp.bfloat16

RS_A = ((0, 640), (1536, 640))
RS_B = ((640, 896), (2176, 896))
CHUNKS = (RS_A[0], RS_B[0], RS_A[1], RS_B[1])
AG_A = ((0, 768), (768, 768))
AG_B = (1536, 1536)

N_GATHER = 2 * (3 + 8) + 8 + 24
N_COPIES = 2 * N_GATHER + 10 + 2 * (8 + 3) + 2 * (3 + 7) + 17 + 1


def kernel(
    d_in, g_in, u_in, ma_in, m1_in, m2_in,
    gg_o, ug_o, ma_o, m1_o, m2_o, w_o,
    d2, gv, uv, mav, m1v, m2v, wg, ht, hr, gr,
    sah, rah, sa, ra, sax, rax, acca, sb, rb, accb, sbz, rbz,
    g, sq, rz, rx, ry, dh, dhs, ob, ggv, ugv,
    ssem, rsem, lsem,
):
    dp, tensor = lax.axis_index("dp"), lax.axis_index("tensor")
    z, x, h = dp // 8, (dp // 2) % 4, dp % 2
    yl, c = tensor // 2, tensor % 2
    y = 2 * h + yl

    def device(zz, xx, yy, cc):
        return (zz * 8 + xx * 2 + yy // 2, (yy % 2) * 2 + cc)

    def at_z(k):
        return device((z + k + 8) % 8, x, y, c)

    def at_x(k):
        return device(z, (x + k + 4) % 4, y, c)

    across = device(z, x, 3 - y, c)
    mate = device(z, x, y, 1 - c)
    pair = (z * 8 + x * 2 + 1 - h, tensor)

    def near(k):
        i = (y * 2 + c + k) % 8
        return device(z, x, i // 2, i % 2)

    count = [0]
    sent = []

    def send(src, dst, to):
        i = count[0]
        count[0] += 1
        copy = pltpu.make_async_remote_copy(
            src_ref=src, dst_ref=dst, send_sem=ssem.at[i], recv_sem=rsem.at[i],
            device_id=to, device_id_type=MESH,
        )
        copy.start()
        sent.append(copy)
        return copy

    def load(src, dst, i):
        copy = pltpu.make_async_copy(src, dst, lsem.at[i])
        copy.start()
        return copy

    load_ma = load(ma_in, mav, 0)
    load_g = load(g_in, gv, 1)
    load_u = load(u_in, uv, 2)
    load_d = load(d_in, d2.at[0], 3)
    load_m1 = load(m1_in, m1v, 4)
    load_m2 = load(m2_in, m2v, 5)

    barrier = pltpu.get_barrier_semaphore()
    friends = (
        [at_z(k) for k in range(1, 8)]
        + [at_x(k) for k in range(1, 4)]
        + [near(k) for k in range(1, 8)]
    )
    for friend in friends:
        pl.semaphore_signal(barrier, inc=1, device_id=friend, device_id_type=MESH)
    load_ma.wait()
    wg[z, x] = mav[...].astype(BF16)
    load_d.wait()
    pl.semaphore_wait(barrier, len(friends))

    class Gather:
        def __init__(self, buf):
            self.buf = buf

        def start(self):
            buf = self.buf
            self.ax = []
            for c0, w in AG_A:
                own = buf.at[z, x, :, pl.ds(c0, w)]
                self.ax.append([send(own, own, at_x(k)) for k in (1, 3, 2)])
            self.bz = [None] * 4
            self.bx = []
            self.az = [[None] * 4 for _ in AG_A]
            self.b_step(1)
            self.b_spread(z)

        def b_spread(self, zz):
            c0, w = AG_B
            block = self.buf.at[zz, x, :, pl.ds(c0, w)]
            self.bx += [send(block, block, at_x(k)) for k in (1, 3, 2)]

        def b_step(self, s):
            c0, w = AG_B
            pieces = ((c0, w), (c0, w)) if s < 4 else ((c0, w // 2), (c0 + w // 2, w // 2))
            up = self.buf.at[(z - s + 9) % 8, x, :, pl.ds(*pieces[0])]
            down = self.buf.at[(z + s - 1) % 8, x, :, pl.ds(*pieces[1])]
            self.bz[s - 1] = [send(up, up, at_z(1)), send(down, down, at_z(-1))]

        def b_next(self, s):
            for copy in self.bz[s - 1]:
                copy.wait_recv()
            if s < 4:
                self.b_step(s + 1)
                self.b_spread((z - s + 8) % 8)
                self.b_spread((z + s) % 8)
            else:
                self.b_spread((z + 4) % 8)

        def a_step(self, j, s):
            cols = pl.ds(*AG_A[j])
            a, b = (pl.ds(0, 4), pl.ds(0, 4)) if s < 4 else (pl.ds(0, 2), pl.ds(2, 2))
            up = self.buf.at[(z - s + 9) % 8, a, :, cols]
            down = self.buf.at[(z + s - 1) % 8, b, :, cols]
            self.az[j][s - 1] = [send(up, up, at_z(1)), send(down, down, at_z(-1))]

        def a_next(self, j, s):
            for copy in self.ax[j] if s == 0 else self.az[j][s - 1]:
                copy.wait_recv()
            if s < 4:
                self.a_step(j, s + 1)

        def finish(self):
            for copy in self.bx:
                copy.wait_recv()

    wga = Gather(wg)
    wga.start()

    half = pl.ds(pl.multiple_of(c * 128, 128), 128)
    cross = [
        send(d2.at[0, half, pl.ds(c0, w)], d2.at[1, half, pl.ds(c0, w)], across)
        for c0, w in CHUNKS
    ]
    swap = [None] * 4

    def pass_on(k):
        cross[k].wait_recv()
        block = d2.at[1, half, pl.ds(*CHUNKS[k])]
        swap[k] = send(block, block, mate)

    load_g.wait()
    load_u.wait()
    for i in range(8):
        cols = pl.ds(i * 128, 128)
        gate = gv[:, cols].astype(F32)
        hidden = gate * jax.nn.sigmoid(gate) * uv[:, cols].astype(F32)
        turned = hidden.astype(BF16).astype(F32).T.astype(BF16)
        for j in range(8):
            ht[j % 2, pl.ds((4 * i + j // 2) * 16, 16), :] = turned[j * 16 : j * 16 + 16, :]
    hid = send(ht.at[1 - h], hr, pair)

    wga.a_next(0, 0)
    wga.a_next(1, 0)
    wga.b_next(1)
    pass_on(0)
    wga.b_next(2)
    pass_on(1)
    wga.a_next(0, 1)
    hid.wait_recv()

    def partial_sums(k):
        c0, w = CHUNKS[k]
        swap[k].wait_recv()
        for i in range(4):
            rows = pl.ds(i * 128, 128)
            acc = jnp.dot(ht[h, rows, :], d2[0, :, pl.ds(c0, w)], preferred_element_type=F32)
            acc += jnp.dot(hr[rows, :], d2[1, :, pl.ds(c0, w)], preferred_element_type=F32)
            gr[pl.ds(2 * i, 2), :, :, pl.ds(c0, w)] = acc.reshape(2, 4, 16, w)

    ring = [[[None, None] for _ in range(4)] for _ in RS_A]
    last_x = [None] * 2

    def a_send(j, s):
        cols = pl.ds(*RS_A[j])
        for way, sign in ((0, 1), (1, -1)):
            to = (z + sign * (5 - s) + 8) % 8
            if s == 1:
                part = pl.ds(2 * way, 2)
                sah[j, way] = gr[to, part, :, cols].astype(BF16)
                ring[j][0][way] = send(sah.at[j, way], rah.at[j, way], at_z(sign))
                continue
            ring[j][s - 2][way].wait_recv()
            if s == 2:
                part, rest = pl.ds(2 * way, 2), pl.ds(2 - 2 * way, 2)
                sa[j, way, 0, part] = (gr[to, part, :, cols] + rah[j, way].astype(F32)).astype(BF16)
                sa[j, way, 0, rest] = gr[to, rest, :, cols].astype(BF16)
            else:
                sa[j, way, s - 2] = (gr[to, :, :, cols] + ra[j, way, s - 3].astype(F32)).astype(BF16)
            ring[j][s - 1][way] = send(sa.at[j, way, s - 2], ra.at[j, way, s - 2], at_z(sign))

    def a_turn(j):
        cols = pl.ds(*RS_A[j])
        for way in (0, 1):
            ring[j][3][way].wait_recv()
        acca[j] = gr[z, :, :, cols] + ra[j, 0, 2].astype(F32) + ra[j, 1, 2].astype(F32)
        last_x[j] = []
        for k in (1, 3, 2):
            sax[j, k - 1] = acca[j, (x + k) % 4].astype(BF16)
            last_x[j].append(send(sax.at[j, k - 1], rax.at[j, k - 1], at_x(k)))

    def a_end(j):
        for copy in last_x[j]:
            copy.wait_recv()
        total = acca[j, x]
        for k in range(3):
            total += rax[j, k].astype(F32)
        g[:, pl.ds(*RS_A[j])] = total

    first_x = [None] * 2
    last_z = [None] * 2

    def b_send(j):
        first_x[j] = []
        for k in (1, 3, 2):
            sb[j, k - 1] = gr[:, (x + k) % 4, :, pl.ds(*RS_B[j])].astype(BF16)
            first_x[j].append(send(sb.at[j, k - 1], rb.at[j, k - 1], at_x(k)))

    def b_turn(j):
        for copy in first_x[j]:
            copy.wait_recv()
        total = gr[:, x, :, pl.ds(*RS_B[j])]
        for k in range(3):
            total += rb[j, k].astype(F32)
        accb[j] = total
        last_z[j] = []
        for k in (4, 3, 5, 2, 6, 1, 7):
            sbz[j, k - 1] = accb[j, (z + k) % 8].astype(BF16)
            last_z[j].append(send(sbz.at[j, k - 1], rbz.at[j, k - 1], at_z(k)))

    def b_end(j):
        for copy in last_z[j]:
            copy.wait_recv()
        total = accb[j, z]
        for k in range(7):
            total += rbz[j, k].astype(F32)
        g[:, pl.ds(*RS_B[j])] = total

    partial_sums(0)
    a_send(0, 1)
    wga.a_next(1, 1)
    wga.b_next(3)
    pass_on(2)
    partial_sums(1)
    b_send(0)
    wga.b_next(4)
    a_send(0, 2)
    wga.a_next(0, 2)
    pass_on(3)
    partial_sums(2)
    a_send(1, 1)
    wga.a_next(1, 2)
    a_send(0, 3)
    partial_sums(3)
    b_send(1)
    a_send(1, 2)
    wga.a_next(0, 3)
    wga.a_next(1, 3)
    a_send(0, 4)
    a_send(1, 3)
    b_turn(0)
    a_turn(0)
    a_send(1, 4)
    b_turn(1)
    a_turn(1)
    b_end(0)
    a_end(0)
    b_end(1)
    a_end(1)

    square = g[...] * g[...]
    square = square[:8] + square[8:]
    total = square[:, 0:128]
    for i in range(1, 24):
        total += square[:, i * 128 : i * 128 + 128]
    sq[0] = total
    load_m1.wait()
    load_m2.wait()
    hops = [send(sq.at[0], rz.at[k - 1], at_z(k)) for k in (4, 3, 5, 2, 6, 1, 7)]

    def d_hidden(j):
        for i in range(4):
            part = lax.dot_general(
                wg[pl.ds(2 * i, 2)].reshape(128, D), d2[j],
                (((1,), (1,)), ((), ())), preferred_element_type=F32,
            )
            if j == 0:
                dh[h, pl.ds(i * 128, 128), :] = part
            else:
                dhs[pl.ds(i * 128, 128), :] = part

    wga.a_next(0, 4)
    wga.a_next(1, 4)
    wga.finish()
    for copy in hops:
        copy.wait_recv()
    for k in range(7):
        total += rz[k]
    sq[1] = total
    hops = [send(sq.at[1], rx.at[k - 1], at_x(k)) for k in (2, 1, 3)]
    d_hidden(1)
    for copy in hops:
        copy.wait_recv()
    for k in range(3):
        total += rx[k]
    sq[2] = total
    hops = [send(sq.at[2], ry.at[k - 1], near(k)) for k in (4, 3, 5, 2, 6, 1, 7)]
    back = send(dhs, dh.at[h], pair)
    d_hidden(0)
    for copy in hops:
        copy.wait_recv()
    for k in range(7):
        total += ry[k]
    factor = 1.0 / jnp.sqrt(jnp.sum(total, keepdims=True) / (FF * D) + 1e-06)

    clipped = g[...] * factor
    first = 0.9 * m1v[...] + 0.1 * clipped
    second = 0.95 * m2v[...] + 0.05 * clipped * clipped
    master = mav[...]
    master = master - 0.003 * (first / (jnp.sqrt(second) + 1e-08) + 0.1 * master)
    mine = pl.ds(pl.multiple_of(h * 16, 16), 16)
    ob[z, x, mine, :] = master.astype(BF16)
    swapped = send(ob.at[z, x, mine], ob.at[z, x, mine], pair)
    mav[...] = master
    m1v[...] = first
    m2v[...] = second
    stores = [load(mav, ma_o, 0), load(m1v, m1_o, 4), load(m2v, m2_o, 5)]
    swapped.wait_recv()

    out = Gather(ob)
    out.start()

    def gradients(i):
        cols = pl.ds(i * 128, 128)
        rows = [dh[j % 2, pl.ds((4 * i + j // 2) * 16, 16), :] for j in range(8)]
        dhid = jnp.concatenate(rows, axis=0).T
        gate = gv[:, cols].astype(F32)
        sig = jax.nn.sigmoid(gate)
        ugv[:, cols] = (dhid * (gate * sig)).astype(BF16)
        ggv[:, cols] = (dhid * uv[:, cols].astype(F32) * sig * (1.0 + gate * (1.0 - sig))).astype(BF16)

    out.a_next(0, 0)
    out.a_next(1, 0)
    out.b_next(1)
    out.b_next(2)
    out.a_next(0, 1)
    out.b_next(3)
    out.a_next(1, 1)
    out.b_next(4)
    back.wait_recv()
    for i in range(4):
        gradients(i)
    out.a_next(0, 2)
    for i in range(4, 8):
        gradients(i)
    stores.append(load(ggv, gg_o, 1))
    stores.append(load(ugv, ug_o, 2))
    out.a_next(1, 2)
    out.a_next(0, 3)
    out.a_next(1, 3)
    out.a_next(0, 4)
    out.a_next(1, 4)
    out.finish()
    stores.append(load(ob, w_o, 3))
    for copy in sent:
        copy.wait_send()
    for copy in stores:
        copy.wait()
    assert count[0] == N_COPIES, count[0]


def on_device(*args):
    vm = pltpu.VMEM
    shape = jax.ShapeDtypeStruct
    anywhere = pl.BlockSpec(memory_space=pl.ANY)
    wa, wb = RS_A[0][1], RS_B[0][1]
    *rest, weight = pl.pallas_call(
        kernel,
        out_shape=(
            shape((256, 1024), BF16),
            shape((256, 1024), BF16),
            shape((16, D), F32),
            shape((16, D), F32),
            shape((16, D), F32),
            shape((8, 4, 32, D), BF16),
        ),
        in_specs=[anywhere] * 6,
        out_specs=(anywhere,) * 6,
        scratch_shapes=[
            vm((2, 256, D), BF16),
            vm((256, 1024), BF16),
            vm((256, 1024), BF16),
            vm((16, D), F32),
            vm((16, D), F32),
            vm((16, D), F32),
            vm((8, 4, 16, D), BF16),
            vm((2, 512, 256), BF16),
            vm((512, 256), BF16),
            vm((8, 4, 16, D), F32),
            vm((2, 2, 2, 16, wa), BF16),
            vm((2, 2, 2, 16, wa), BF16),
            vm((2, 2, 3, 4, 16, wa), BF16),
            vm((2, 2, 3, 4, 16, wa), BF16),
            vm((2, 3, 16, wa), BF16),
            vm((2, 3, 16, wa), BF16),
            vm((2, 4, 16, wa), F32),
            vm((2, 3, 8, 16, wb), BF16),
            vm((2, 3, 8, 16, wb), BF16),
            vm((2, 8, 16, wb), F32),
            vm((2, 7, 16, wb), BF16),
            vm((2, 7, 16, wb), BF16),
            vm((16, D), F32),
            vm((3, 8, 128), F32),
            vm((7, 8, 128), F32),
            vm((3, 8, 128), F32),
            vm((7, 8, 128), F32),
            vm((2, 512, 256), F32),
            vm((512, 256), F32),
            vm((8, 4, 32, D), BF16),
            vm((256, 1024), BF16),
            vm((256, 1024), BF16),
            pltpu.SemaphoreType.DMA((N_COPIES,)),
            pltpu.SemaphoreType.DMA((N_COPIES,)),
            pltpu.SemaphoreType.DMA((6,)),
        ],
        compiler_params=pltpu.CompilerParams(
            collective_id=0, has_side_effects=True, vmem_limit_bytes=48 << 20
        ),
        name="step",
    )(*args)
    return (*rest, weight.reshape(1024, D))


def solution(mesh):
    rows = P(("tensor", "dp"), None)
    both = P("dp", "tensor")
    return jax.shard_map(
        on_device,
        mesh=mesh,
        in_specs=(P("dp", None), both, both, rows, rows, rows),
        out_specs=(both, both, rows, rows, rows, P("tensor", None)),
        check_vma=False,
    )
```

```python
import functools

import jax
import jax.numpy as jnp
from jax import lax
from jax.experimental import pallas as pl
from jax.experimental.pallas import tpu as pltpu
from jax.sharding import PartitionSpec as P

D = 3072
FF = 4096
MESH = pl.DeviceIdType.MESH
F32 = jnp.float32
BF16 = jnp.bfloat16

RS_A = ((1024, 768), (2304, 768))
RS_B = ((0, 1024), (1792, 512))
CHUNKS = (RS_B[0], RS_A[0], RS_B[1], RS_A[1])
W_A = ((0, 768), (768, 768))
W_B = (1536, 1536)
N_C = ((0, 640), (640, 640))
N_A = (1280, 640)
N_B = (1920, 1152)
N_SWAP = (1280, 1792)

N_COPIES = (2 * 11 + 32) + 18 + 2 * (8 + 3) + 2 * (3 + 7) + 17 + 1 + 2 * 19 + 11 + 32


def kernel(
    d_in, g_in, u_in, ma_in, m1_in, m2_in,
    ggv, ugv, ma_o, m1_o, m2_o, ob,
    d2, gv, uv, mav, m1v, m2v, wg, ht, hr, gr,
    sah, rah, sa, ra, sax, rax, acca,
    sb0, rb0, accb0, sbz0, rbz0, sb1, rb1, accb1, sbz1, rbz1,
    g, sq, rz, rx, ry, dh, dhs, dhr, dht,
    ssem, rsem, lsem,
):
    dp, tensor = lax.axis_index("dp"), lax.axis_index("tensor")
    z, x, h = dp // 8, (dp // 2) % 4, dp % 2
    yl, c = tensor // 2, tensor % 2
    y = 2 * h + yl

    def device(zz, xx, yy, cc):
        return (zz * 8 + xx * 2 + yy // 2, (yy % 2) * 2 + cc)

    def at_z(k):
        return device((z + k + 8) % 8, x, y, c)

    def at_x(k):
        return device(z, (x + k + 4) % 4, y, c)

    sb, rb, accb, sbz, rbz = (sb0, sb1), (rb0, rb1), (accb0, accb1), (sbz0, sbz1), (rbz0, rbz1)
    across = device(z, x, 3 - y, c)
    beside = device(z, x, 2 * h + 1 - yl, c)
    mate = device(z, x, y, 1 - c)
    pair = (z * 8 + x * 2 + 1 - h, tensor)

    def near(k):
        i = (y * 2 + c + k) % 8
        return device(z, x, i // 2, i % 2)

    count = [0]
    sent = []

    def send(src, dst, to):
        i = count[0]
        count[0] += 1
        copy = pltpu.make_async_remote_copy(
            src_ref=src, dst_ref=dst, send_sem=ssem.at[i], recv_sem=rsem.at[i],
            device_id=to, device_id_type=MESH,
        )
        copy.start()
        sent.append(copy)
        return copy

    def load(src, dst, i):
        copy = pltpu.make_async_copy(src, dst, lsem.at[i])
        copy.start()
        return copy

    load_ma = load(ma_in, mav, 0)
    load_g = load(g_in, gv, 1)
    load_u = load(u_in, uv, 2)
    load_d = load(d_in, d2.at[0], 3)
    load_m1 = load(m1_in, m1v, 4)
    load_m2 = load(m2_in, m2v, 5)

    barrier = pltpu.get_barrier_semaphore()
    friends = (
        [at_z(k) for k in range(1, 8)]
        + [at_x(k) for k in range(1, 4)]
        + [near(k) for k in range(1, 8)]
    )
    for friend in friends:
        pl.semaphore_signal(barrier, inc=1, device_id=friend, device_id_type=MESH)
    load_ma.wait()
    wg[z, x] = mav[...].astype(BF16)
    pl.semaphore_wait(barrier, len(friends))

    class AlongXZ:
        def __init__(self, buf, rows, cols, to_pair=False):
            self.buf, self.rows, self.cols, self.to_pair = buf, rows, pl.ds(*cols), to_pair
            self.paired = []

        def start(self):
            own = self.buf.at[z, x, self.rows, self.cols]
            self.got = [send(own, own, at_x(k)) for k in (1, 3, 2)]

        def forward(self, block):
            if self.to_pair:
                self.paired.append(send(block, block, pair))

        def next(self, s):
            for copy in self.got:
                copy.wait_recv()
            a, b = (pl.ds(0, 4), pl.ds(0, 4)) if s < 3 else (pl.ds(0, 2), pl.ds(2, 2))
            if s < 4:
                up = self.buf.at[(z - s + 8) % 8, a, self.rows, self.cols]
                down = self.buf.at[(z + s) % 8, b, self.rows, self.cols]
                self.got = [send(up, up, at_z(1)), send(down, down, at_z(-1))]
            for k, part in ((-s, pl.ds(0, 4)), (s, pl.ds(0, 4)))[s == 0 :] if s < 4 else ((4, pl.ds(0, 4)),):
                self.forward(self.buf.at[(z + k + 8) % 8, part, self.rows, self.cols])

        def finish(self):
            for copy in self.paired:
                copy.wait_recv()

    class AlongZX:
        def __init__(self, buf, rows, cols):
            self.buf, self.rows, self.cols = buf, rows, cols
            self.spread = []

        def start(self):
            self.along_x(z)
            self.along_z(1)

        def along_x(self, zz):
            block = self.buf.at[zz, x, self.rows, pl.ds(*self.cols)]
            self.spread += [send(block, block, at_x(k)) for k in (1, 3, 2)]

        def along_z(self, s):
            c0, w = self.cols
            a, b = ((c0, w), (c0, w)) if s < 4 else ((c0, w // 2), (c0 + w // 2, w // 2))
            if s == 4 and w % 256:
                a, b = (c0, w // 2 - 64), (c0 + w // 2 - 64, w // 2 + 64)
            up = self.buf.at[(z - s + 9) % 8, x, self.rows, pl.ds(*a)]
            down = self.buf.at[(z + s - 1) % 8, x, self.rows, pl.ds(*b)]
            self.got = [send(up, up, at_z(1)), send(down, down, at_z(-1))]

        def next(self, s):
            for copy in self.got:
                copy.wait_recv()
            if s < 4:
                self.along_z(s + 1)
                self.along_x((z - s + 8) % 8)
                self.along_x((z + s) % 8)
            else:
                self.along_x((z + 4) % 8)

        def finish(self):
            for copy in self.spread:
                copy.wait_recv()

    everything = pl.ds(0, 16)
    w_a = [AlongXZ(wg, everything, cols) for cols in W_A]
    w_b = AlongZX(wg, everything, W_B)
    w_a[0].start()
    w_a[1].start()

    load_d.wait()
    theirs = pl.ds(pl.multiple_of((1 - yl) * 128 + c * 64, 64), 64)
    mine = pl.ds(pl.multiple_of(yl * 128 + c * 64, 64), 64)
    cross, side, swap = [None] * 4, [None] * 4, [[] for _ in range(4)]

    def take(k):
        cols = pl.ds(*CHUNKS[k])
        cross[k] = send(d2.at[0, theirs, cols], d2.at[1, theirs, cols], across)

    def pass_on(k):
        cross[k].wait_recv()
        block = d2.at[1, mine, pl.ds(*CHUNKS[k])]
        side[k] = send(block, block, beside)
        swap[k].append(send(block, block, mate))

    def pass_on_again(k):
        side[k].wait_recv()
        block = d2.at[1, theirs, pl.ds(*CHUNKS[k])]
        swap[k].append(send(block, block, mate))

    take(0)
    take(1)
    w_b.start()

    load_g.wait()
    load_u.wait()
    for i in range(8):
        cols = pl.ds(i * 128, 128)
        gate = gv[:, cols].astype(F32)
        hidden = gate * jax.nn.sigmoid(gate) * uv[:, cols].astype(F32)
        turned = hidden.astype(BF16).astype(F32).T.astype(BF16)
        for j in range(8):
            ht[j % 2, pl.ds((4 * i + j // 2) * 16, 16), :] = turned[j * 16 : j * 16 + 16, :]
    hid = send(ht.at[1 - h], hr, pair)

    take(2)
    take(3)
    w_a[0].next(0)
    w_a[1].next(0)
    pass_on(0)
    w_b.next(1)
    pass_on(1)
    w_b.next(2)
    pass_on_again(0)
    pass_on(2)
    w_a[0].next(1)
    pass_on_again(1)
    pass_on(3)
    w_a[1].next(1)
    hid.wait_recv()

    def partial_sums(k):
        c0, w = CHUNKS[k]
        for copy in swap[k]:
            copy.wait_recv()
        for i in range(w // 256):
            cols = pl.ds(c0 + i * 256, 256)
            acc = jnp.dot(ht[h], d2[0, :, cols], preferred_element_type=F32)
            acc += jnp.dot(hr[...], d2[1, :, cols], preferred_element_type=F32)
            gr[:, :, :, cols] = acc.reshape(8, 4, 16, 256)

    ring = [[[None, None] for _ in range(4)] for _ in RS_A]
    last_x = [None] * 2

    def a_send(j, s):
        cols = pl.ds(*RS_A[j])
        for way, sign in ((0, 1), (1, -1)):
            to = (z + sign * (5 - s) + 8) % 8
            if s == 1:
                part = pl.ds(2 * way, 2)
                sah[j, way] = gr[to, part, :, cols].astype(BF16)
                ring[j][0][way] = send(sah.at[j, way], rah.at[j, way], at_z(sign))
                continue
            ring[j][s - 2][way].wait_recv()
            if s == 2:
                part, rest = pl.ds(2 * way, 2), pl.ds(2 - 2 * way, 2)
                sa[j, way, 0, part] = (gr[to, part, :, cols] + rah[j, way].astype(F32)).astype(BF16)
                sa[j, way, 0, rest] = gr[to, rest, :, cols].astype(BF16)
            else:
                sa[j, way, s - 2] = (gr[to, :, :, cols] + ra[j, way, s - 3].astype(F32)).astype(BF16)
            ring[j][s - 1][way] = send(sa.at[j, way, s - 2], ra.at[j, way, s - 2], at_z(sign))

    def a_turn(j):
        cols = pl.ds(*RS_A[j])
        for way in (0, 1):
            ring[j][3][way].wait_recv()
        acca[j] = gr[z, :, :, cols] + ra[j, 0, 2].astype(F32) + ra[j, 1, 2].astype(F32)
        last_x[j] = []
        for k in (1, 3, 2):
            sax[j, k - 1] = acca[j, (x + k) % 4].astype(BF16)
            last_x[j].append(send(sax.at[j, k - 1], rax.at[j, k - 1], at_x(k)))

    def a_end(j):
        for copy in last_x[j]:
            copy.wait_recv()
        total = acca[j, x]
        for k in range(3):
            total += rax[j, k].astype(F32)
        g[:, pl.ds(*RS_A[j])] = total

    first_x = [None] * 2
    last_z = [None] * 2

    def b_send(j):
        first_x[j] = []
        for k in (1, 3, 2):
            sb[j][k - 1] = gr[:, (x + k) % 4, :, pl.ds(*RS_B[j])].astype(BF16)
            first_x[j].append(send(sb[j].at[k - 1], rb[j].at[k - 1], at_x(k)))

    def b_turn(j):
        for copy in first_x[j]:
            copy.wait_recv()
        total = gr[:, x, :, pl.ds(*RS_B[j])]
        for k in range(3):
            total += rb[j][k].astype(F32)
        accb[j][...] = total
        last_z[j] = []
        for k in (4, 3, 5, 2, 6, 1, 7):
            sbz[j][k - 1] = accb[j][(z + k) % 8].astype(BF16)
            last_z[j].append(send(sbz[j].at[k - 1], rbz[j].at[k - 1], at_z(k)))

    def b_end(j):
        for copy in last_z[j]:
            copy.wait_recv()
        total = accb[j][z]
        for k in range(7):
            total += rbz[j][k].astype(F32)
        g[:, pl.ds(*RS_B[j])] = total

    partial_sums(0)
    b_send(0)
    partial_sums(1)
    a_send(0, 1)
    pass_on_again(2)
    pass_on_again(3)
    w_b.next(3)
    partial_sums(2)
    b_send(1)
    a_send(0, 2)
    partial_sums(3)
    a_send(1, 1)
    a_send(0, 3)
    a_send(1, 2)
    b_turn(0)
    a_send(0, 4)
    a_send(1, 3)
    b_turn(1)
    a_turn(0)
    a_send(1, 4)
    w_b.next(4)
    w_a[0].next(2)
    a_turn(1)
    w_a[1].next(2)
    b_end(0)
    a_end(0)
    b_end(1)
    a_end(1)

    square = g[...] * g[...]
    square = square[:8] + square[8:]
    total = square[:, 0:128]
    for i in range(1, 24):
        total += square[:, i * 128 : i * 128 + 128]
    sq[0] = total
    load_m1.wait()
    load_m2.wait()
    hops = [send(sq.at[0], rz.at[k - 1], at_z(k)) for k in (4, 3, 5, 2, 6, 1, 7)]

    def d_hidden(j):
        acc = None
        for i in range(6):
            cols = pl.ds(i * 512, 512)
            part = lax.dot_general(
                wg[:, :, :, cols].reshape(512, 512), d2[j, :, cols],
                (((1,), (1,)), ((), ())), preferred_element_type=F32,
            )
            acc = part if acc is None else acc + part
        if j == 0:
            dh[...] = acc
        else:
            dhs[...] = acc.astype(BF16)

    w_a[0].next(3)
    w_a[1].next(3)
    for copy in hops:
        copy.wait_recv()
    for k in range(7):
        total += rz[k]
    sq[1] = total
    hops = [send(sq.at[1], rx.at[k - 1], at_x(k)) for k in (2, 1, 3)]
    w_a[0].next(4)
    w_a[1].next(4)
    for copy in hops:
        copy.wait_recv()
    for k in range(3):
        total += rx[k]
    sq[2] = total
    hops = [send(sq.at[2], ry.at[k - 1], near(k)) for k in (4, 3, 5, 2, 6, 1, 7)]
    w_b.finish()
    d_hidden(1)
    back = send(dhs, dhr, pair)
    for copy in hops:
        copy.wait_recv()
    for k in range(7):
        total += ry[k]
    factor = 1.0 / jnp.sqrt(jnp.sum(total, keepdims=True) / (FF * D) + 1e-06)

    clipped = g[...] * factor
    first = 0.9 * m1v[...] + 0.1 * clipped
    second = 0.95 * m2v[...] + 0.05 * clipped * clipped
    master = mav[...]
    master = master - 0.003 * (first / (jnp.sqrt(second) + 1e-08) + 0.1 * master)
    own = pl.ds(pl.multiple_of(h * 16, 16), 16)
    ob[z, x, own, :] = master.astype(BF16)

    n_c = [AlongXZ(ob, own, cols, to_pair=True) for cols in N_C]
    n_a = AlongXZ(ob, pl.ds(0, 32), N_A)
    n_b = AlongZX(ob, pl.ds(0, 32), N_B)
    block = ob.at[z, x, own, pl.ds(*N_SWAP)]
    n_c[0].start()
    swapped = send(block, block, pair)
    n_c[1].start()
    ma_o[...] = master
    m1_o[...] = first
    m2_o[...] = second

    def gradients(i):
        cols = pl.ds(i * 128, 128)
        rows = [dht[j % 2, pl.ds((4 * i + j // 2) * 16, 16), :] for j in range(8)]
        dhid = jnp.concatenate(rows, axis=0).T
        gate = gv[:, cols].astype(F32)
        sig = jax.nn.sigmoid(gate)
        ugv[:, cols] = (dhid * (gate * sig)).astype(BF16)
        ggv[:, cols] = (dhid * uv[:, cols].astype(F32) * sig * (1.0 + gate * (1.0 - sig))).astype(BF16)

    n_c[0].next(0)
    n_c[1].next(0)
    swapped.wait_recv()
    n_a.start()
    n_b.start()
    d_hidden(0)
    n_c[0].next(1)
    n_c[1].next(1)
    n_b.next(1)
    n_a.next(0)
    n_b.next(2)
    n_c[0].next(2)
    n_c[1].next(2)
    n_b.next(3)
    n_a.next(1)
    n_b.next(4)
    n_c[0].next(3)
    n_c[1].next(3)
    n_a.next(2)
    back.wait_recv()
    dht[h] = dh[...]
    dht[1 - h] = dhr[...].astype(F32)
    for i in range(4):
        gradients(i)
    n_c[0].next(4)
    n_c[1].next(4)
    n_a.next(3)
    for i in range(4, 8):
        gradients(i)
    n_a.next(4)
    n_b.finish()
    n_c[0].finish()
    n_c[1].finish()
    for copy in sent:
        copy.wait_send()
    assert count[0] == N_COPIES, (count[0], N_COPIES)


def store(*refs):
    sem = refs[-1]
    copies = [pltpu.make_async_copy(refs[i], refs[6 + i], sem.at[i]) for i in (5, 0, 1, 2, 3, 4)]
    for copy in copies:
        copy.start()
    for copy in copies:
        copy.wait()


def on_device(*args):
    vm = pltpu.VMEM
    shape = jax.ShapeDtypeStruct
    inside = pl.BlockSpec(memory_space=pltpu.VMEM)
    outside = pl.BlockSpec(memory_space=pltpu.HBM)
    wa = RS_A[0][1]
    shapes = (
        ((256, 1024), BF16), ((256, 1024), BF16), ((16, D), F32), ((16, D), F32), ((16, D), F32), ((8, 4, 32, D), BF16)
    )
    results = pl.pallas_call(
        kernel,
        out_shape=tuple(vm(*leaf) for leaf in shapes),
        in_specs=[outside] * 6,
        out_specs=(inside,) * 6,
        scratch_shapes=[
            vm((2, 256, D), BF16),
            vm((256, 1024), BF16),
            vm((256, 1024), BF16),
            vm((16, D), F32),
            vm((16, D), F32),
            vm((16, D), F32),
            vm((8, 4, 16, D), BF16),
            vm((2, 512, 256), BF16),
            vm((512, 256), BF16),
            vm((8, 4, 16, D), F32),
            vm((2, 2, 2, 16, wa), BF16),
            vm((2, 2, 2, 16, wa), BF16),
            vm((2, 2, 3, 4, 16, wa), BF16),
            vm((2, 2, 3, 4, 16, wa), BF16),
            vm((2, 3, 16, wa), BF16),
            vm((2, 3, 16, wa), BF16),
            vm((2, 4, 16, wa), F32),
            *(
                vm(leaf, kind)
                for _, wb in RS_B
                for leaf, kind in (
                    ((3, 8, 16, wb), BF16), ((3, 8, 16, wb), BF16), ((8, 16, wb), F32),
                    ((7, 16, wb), BF16), ((7, 16, wb), BF16),
                )
            ),
            vm((16, D), F32),
            vm((3, 8, 128), F32),
            vm((7, 8, 128), F32),
            vm((3, 8, 128), F32),
            vm((7, 8, 128), F32),
            vm((512, 256), F32),
            vm((512, 256), BF16),
            vm((512, 256), BF16),
            vm((2, 512, 256), F32),
            pltpu.SemaphoreType.DMA((N_COPIES,)),
            pltpu.SemaphoreType.DMA((N_COPIES,)),
            pltpu.SemaphoreType.DMA((6,)),
        ],
        compiler_params=pltpu.CompilerParams(
            collective_id=0, has_side_effects=True, vmem_limit_bytes=48 << 20
        ),
        name="step",
    )(*args)
    *rest, weight = pl.pallas_call(
        store,
        out_shape=tuple(shape(*leaf) for leaf in shapes),
        in_specs=[inside] * 6,
        out_specs=(outside,) * 6,
        scratch_shapes=[pltpu.SemaphoreType.DMA((6,))],
        compiler_params=pltpu.CompilerParams(vmem_limit_bytes=1 << 20),
        name="store",
    )(*(pltpu.with_memory_space_constraint(leaf, pltpu.VMEM) for leaf in results))
    return (*rest, weight.reshape(1024, D))


def solution(mesh):
    rows = P(("tensor", "dp"), None)
    both = P("dp", "tensor")
    return jax.shard_map(
        on_device,
        mesh=mesh,
        in_specs=(P("dp", None), both, both, rows, rows, rows),
        out_specs=(both, both, rows, rows, rows, P("tensor", None)),
        check_vma=False,
    )
```

```python
import functools

import jax
import jax.numpy as jnp
from jax import lax
from jax.experimental import pallas as pl
from jax.experimental.pallas import tpu as pltpu
from jax.sharding import PartitionSpec as P

D = 3072
FF = 4096
MESH = pl.DeviceIdType.MESH
F32 = jnp.float32
BF16 = jnp.bfloat16

RS_A = ((1024, 768), (2304, 768))
RS_B = ((0, 1024), (1792, 512))
CHUNKS = (RS_B[0], RS_A[0], RS_B[1], RS_A[1])
W_A = ((0, 768), (768, 768))
W_B = (1536, 1536)
N_C = ((0, 640), (640, 640))
N_A = (1280, 640)
N_B = (1920, 1152)
N_SWAP = (1280, 1792)

N_COPIES = (2 * 11 + 32) + 18 + 2 * (8 + 3) + 2 * (3 + 7) + 17 + 1 + 2 * 19 + 11 + 2 * 32


def kernel(
    d_in, g_in, u_in, ma_in, m1_in, m2_in,
    ggv, ugv, ma_o, m1_o, m2_o, ob,
    d2, gv, uv, mav, m1v, m2v, wg, ht, hr, gr,
    sah, rah, sa, ra, sax, rax, acca,
    sb0, rb0, accb0, sbz0, rbz0, sb1, rb1, accb1, sbz1, rbz1,
    g, sq, rz, rx, ry, dh, dhs, dhr, dht,
    ssem, rsem, lsem,
):
    dp, tensor = lax.axis_index("dp"), lax.axis_index("tensor")
    z, x, h = dp // 8, (dp // 2) % 4, dp % 2
    yl, c = tensor // 2, tensor % 2
    y = 2 * h + yl

    def device(zz, xx, yy, cc):
        return (zz * 8 + xx * 2 + yy // 2, (yy % 2) * 2 + cc)

    def at_z(k):
        return device((z + k + 8) % 8, x, y, c)

    def at_x(k):
        return device(z, (x + k + 4) % 4, y, c)

    sb, rb, accb, sbz, rbz = (sb0, sb1), (rb0, rb1), (accb0, accb1), (sbz0, sbz1), (rbz0, rbz1)
    across = device(z, x, 3 - y, c)
    beside = device(z, x, 2 * h + 1 - yl, c)
    mate = device(z, x, y, 1 - c)
    pair = (z * 8 + x * 2 + 1 - h, tensor)

    def near(k):
        i = (y * 2 + c + k) % 8
        return device(z, x, i // 2, i % 2)

    count = [0]
    sent = []

    def send(src, dst, to):
        i = count[0]
        count[0] += 1
        copy = pltpu.make_async_remote_copy(
            src_ref=src, dst_ref=dst, send_sem=ssem.at[i], recv_sem=rsem.at[i],
            device_id=to, device_id_type=MESH,
        )
        copy.start()
        sent.append(copy)
        return copy

    def load(src, dst, i):
        copy = pltpu.make_async_copy(src, dst, lsem.at[i])
        copy.start()
        return copy

    load_ma = load(ma_in, mav, 0)
    load_g = load(g_in, gv, 1)
    load_u = load(u_in, uv, 2)
    load_d = load(d_in, d2.at[0], 3)
    load_m1 = load(m1_in, m1v, 4)
    load_m2 = load(m2_in, m2v, 5)

    barrier = pltpu.get_barrier_semaphore()
    friends = (
        [at_z(k) for k in range(1, 8)]
        + [at_x(k) for k in range(1, 4)]
        + [near(k) for k in range(1, 8)]
    )
    for friend in friends:
        pl.semaphore_signal(barrier, inc=1, device_id=friend, device_id_type=MESH)
    load_ma.wait()
    wg[z, x] = mav[...].astype(BF16)
    pl.semaphore_wait(barrier, len(friends))

    class AlongXZ:
        def __init__(self, buf, rows, cols, to_pair=False):
            self.buf, self.rows, self.cols, self.to_pair = buf, rows, pl.ds(*cols), to_pair
            self.paired = []

        def start(self):
            own = self.buf.at[z, x, self.rows, self.cols]
            self.got = [send(own, own, at_x(k)) for k in (1, 3, 2)]

        def forward(self, block):
            if self.to_pair:
                self.paired.append(send(block, block, pair))

        def next(self, s):
            for copy in self.got:
                copy.wait_recv()
            a, b = (pl.ds(0, 4), pl.ds(0, 4)) if s < 3 else (pl.ds(0, 2), pl.ds(2, 2))
            if s < 4:
                up = self.buf.at[(z - s + 8) % 8, a, self.rows, self.cols]
                down = self.buf.at[(z + s) % 8, b, self.rows, self.cols]
                self.got = [send(up, up, at_z(1)), send(down, down, at_z(-1))]
            for k, part in ((-s, pl.ds(0, 4)), (s, pl.ds(0, 4)))[s == 0 :] if s < 4 else ((4, pl.ds(0, 4)),):
                self.forward(self.buf.at[(z + k + 8) % 8, part, self.rows, self.cols])

        def finish(self):
            for copy in self.paired:
                copy.wait_recv()

    class AlongZX:
        def __init__(self, buf, rows, cols):
            self.buf, self.rows, self.cols = buf, rows, cols
            self.spread = []

        def start(self):
            self.along_x(z)
            self.along_z(1)

        def along_x(self, zz):
            block = self.buf.at[zz, x, self.rows, pl.ds(*self.cols)]
            self.spread += [send(block, block, at_x(k)) for k in (1, 3, 2)]

        def along_z(self, s):
            c0, w = self.cols
            a, b = ((c0, w), (c0, w)) if s < 4 else ((c0, w // 2), (c0 + w // 2, w // 2))
            if s == 4 and w % 256:
                a, b = (c0, w // 2 - 64), (c0 + w // 2 - 64, w // 2 + 64)
            up = self.buf.at[(z - s + 9) % 8, x, self.rows, pl.ds(*a)]
            down = self.buf.at[(z + s - 1) % 8, x, self.rows, pl.ds(*b)]
            self.got = [send(up, up, at_z(1)), send(down, down, at_z(-1))]

        def next(self, s):
            for copy in self.got:
                copy.wait_recv()
            if s < 4:
                self.along_z(s + 1)
                self.along_x((z - s + 8) % 8)
                self.along_x((z + s) % 8)
            else:
                self.along_x((z + 4) % 8)

        def finish(self):
            for copy in self.spread:
                copy.wait_recv()

    everything = pl.ds(0, 16)
    w_a = [AlongXZ(wg, everything, cols) for cols in W_A]
    w_b = AlongZX(wg, everything, W_B)
    theirs = pl.ds(pl.multiple_of((1 - yl) * 128 + c * 64, 64), 64)
    mine = pl.ds(pl.multiple_of(yl * 128 + c * 64, 64), 64)
    cross, side, swap = [None] * 4, [None] * 4, [[] for _ in range(4)]

    def take(k):
        if k == 0:
            load_d.wait()
        cols = pl.ds(*CHUNKS[k])
        cross[k] = send(d2.at[0, theirs, cols], d2.at[1, theirs, cols], across)

    def pass_on(k):
        cross[k].wait_recv()
        block = d2.at[1, mine, pl.ds(*CHUNKS[k])]
        side[k] = send(block, block, beside)
        swap[k].append(send(block, block, mate))

    def pass_on_again(k):
        side[k].wait_recv()
        block = d2.at[1, theirs, pl.ds(*CHUNKS[k])]
        swap[k].append(send(block, block, mate))

    hid = []

    def hide():
        load_g.wait()
        load_u.wait()
        for i in range(8):
            cols = pl.ds(i * 128, 128)
            gate = gv[:, cols].astype(F32)
            hidden = gate * jax.nn.sigmoid(gate) * uv[:, cols].astype(F32)
            turned = hidden.astype(BF16).astype(F32).T.astype(BF16)
            for j in range(8):
                ht[j % 2, pl.ds((4 * i + j // 2) * 16, 16), :] = turned[j * 16 : j * 16 + 16, :]
        hid.append(send(ht.at[1 - h], hr, pair))

    def partial_sums(k):
        c0, w = CHUNKS[k]
        if k == 0:
            hid[0].wait_recv()
        for copy in swap[k]:
            copy.wait_recv()
        for i in range(w // 256):
            cols = pl.ds(c0 + i * 256, 256)
            acc = jnp.dot(ht[h], d2[0, :, cols], preferred_element_type=F32)
            acc += jnp.dot(hr[...], d2[1, :, cols], preferred_element_type=F32)
            gr[:, :, :, cols] = acc.reshape(8, 4, 16, 256)

    ring = [[[None, None] for _ in range(4)] for _ in RS_A]
    last_x = [None] * 2

    def a_send(j, s):
        cols = pl.ds(*RS_A[j])
        for way, sign in ((0, 1), (1, -1)):
            to = (z + sign * (5 - s) + 8) % 8
            if s == 1:
                part = pl.ds(2 * way, 2)
                sah[j, way] = gr[to, part, :, cols].astype(BF16)
                ring[j][0][way] = send(sah.at[j, way], rah.at[j, way], at_z(sign))
                continue
            ring[j][s - 2][way].wait_recv()
            if s == 2:
                part, rest = pl.ds(2 * way, 2), pl.ds(2 - 2 * way, 2)
                sa[j, way, 0, part] = (gr[to, part, :, cols] + rah[j, way].astype(F32)).astype(BF16)
                sa[j, way, 0, rest] = gr[to, rest, :, cols].astype(BF16)
            else:
                sa[j, way, s - 2] = (gr[to, :, :, cols] + ra[j, way, s - 3].astype(F32)).astype(BF16)
            ring[j][s - 1][way] = send(sa.at[j, way, s - 2], ra.at[j, way, s - 2], at_z(sign))

    def a_turn(j):
        cols = pl.ds(*RS_A[j])
        for way in (0, 1):
            ring[j][3][way].wait_recv()
        acca[j] = gr[z, :, :, cols] + ra[j, 0, 2].astype(F32) + ra[j, 1, 2].astype(F32)
        last_x[j] = []
        for k in (1, 3, 2):
            sax[j, k - 1] = acca[j, (x + k) % 4].astype(BF16)
            last_x[j].append(send(sax.at[j, k - 1], rax.at[j, k - 1], at_x(k)))

    def a_end(j):
        for copy in last_x[j]:
            copy.wait_recv()
        total = acca[j, x]
        for k in range(3):
            total += rax[j, k].astype(F32)
        g[:, pl.ds(*RS_A[j])] = total

    first_x = [None] * 2
    last_z = [None] * 2

    def b_send(j):
        first_x[j] = []
        for k in (1, 3, 2):
            sb[j][k - 1] = gr[:, (x + k) % 4, :, pl.ds(*RS_B[j])].astype(BF16)
            first_x[j].append(send(sb[j].at[k - 1], rb[j].at[k - 1], at_x(k)))

    def b_turn(j):
        for copy in first_x[j]:
            copy.wait_recv()
        total = gr[:, x, :, pl.ds(*RS_B[j])]
        for k in range(3):
            total += rb[j][k].astype(F32)
        accb[j][...] = total
        last_z[j] = []
        for k in (4, 3, 5, 2, 6, 1, 7):
            sbz[j][k - 1] = accb[j][(z + k) % 8].astype(BF16)
            last_z[j].append(send(sbz[j].at[k - 1], rbz[j].at[k - 1], at_z(k)))

    def b_end(j):
        for copy in last_z[j]:
            copy.wait_recv()
        total = accb[j][z]
        for k in range(7):
            total += rbz[j][k].astype(F32)
        g[:, pl.ds(*RS_B[j])] = total

    rounds = []

    def exchange(i, dst, hops):
        rounds.append([send(sq.at[i], dst.at[k - 1], to(k)) for k, to in hops])

    def arrived(i, dst, n):
        for copy in rounds[i]:
            copy.wait_recv()
        total = sq[i]
        for k in range(n):
            total += dst[k]
        return total

    def squares():
        square = g[...] * g[...]
        square = square[:8] + square[8:]
        total = square[:, 0:128]
        for i in range(1, 24):
            total += square[:, i * 128 : i * 128 + 128]
        sq[0] = total
        exchange(0, rz, [(k, at_z) for k in (4, 3, 5, 2, 6, 1, 7)])

    def squares_x():
        sq[1] = arrived(0, rz, 7)
        exchange(1, rx, [(k, at_x) for k in (2, 1, 3)])

    def squares_y():
        sq[2] = arrived(1, rx, 3)
        exchange(2, ry, [(k, near) for k in (4, 3, 5, 2, 6, 1, 7)])

    back = []

    def d_hidden(j):
        if j == 1:
            w_b.finish()
        acc = None
        for i in range(6):
            cols = pl.ds(i * 512, 512)
            part = lax.dot_general(
                wg[:, :, :, cols].reshape(512, 512), d2[j, :, cols],
                (((1,), (1,)), ((), ())), preferred_element_type=F32,
            )
            acc = part if acc is None else acc + part
        if j == 0:
            dh[...] = acc
        else:
            dhs[...] = acc.astype(BF16)
            back.append(send(dhs, dhr, pair))

    own, other = (pl.ds(pl.multiple_of(i * 16, 16), 16) for i in (h, 1 - h))

    def adam():
        load_m1.wait()
        load_m2.wait()
        total = arrived(2, ry, 7)
        factor = 1.0 / jnp.sqrt(jnp.sum(total, keepdims=True) / (FF * D) + 1e-06)
        clipped = g[...] * factor
        first = 0.9 * m1v[...] + 0.1 * clipped
        second = 0.95 * m2v[...] + 0.05 * clipped * clipped
        master = mav[...]
        master = master - 0.003 * (first / (jnp.sqrt(second) + 1e-08) + 0.1 * master)
        ob[z, x, own, :] = master.astype(BF16)
        ma_o[...] = master
        m1_o[...] = first
        m2_o[...] = second

    n_c = [AlongXZ(ob, own, cols, to_pair=True) for cols in N_C]
    n_a = AlongXZ(ob, pl.ds(0, 32), N_A)
    n_b = [AlongZX(ob, rows, N_B) for rows in (own, other)]
    swapped = []

    def swap_rows():
        block = ob.at[z, x, own, pl.ds(*N_SWAP)]
        swapped.append(send(block, block, pair))

    def swapped_rows():
        swapped[0].wait_recv()
        n_a.start()

    def turn_back():
        back[0].wait_recv()
        dht[h] = dh[...]
        dht[1 - h] = dhr[...].astype(F32)

    def gradients(i):
        cols = pl.ds(i * 128, 128)
        rows = [dht[j % 2, pl.ds((4 * i + j // 2) * 16, 16), :] for j in range(8)]
        dhid = jnp.concatenate(rows, axis=0).T
        gate = gv[:, cols].astype(F32)
        sig = jax.nn.sigmoid(gate)
        ugv[:, cols] = (dhid * (gate * sig)).astype(BF16)
        ggv[:, cols] = (dhid * uv[:, cols].astype(F32) * sig * (1.0 + gate * (1.0 - sig))).astype(BF16)

    take(0)
    w_b.start()
    hide()
    w_a[1].start()
    w_a[0].start()
    w_a[0].next(0)
    take(1)
    w_b.next(1)
    take(2)
    take(3)
    pass_on(0)
    w_a[1].next(0)
    w_a[0].next(1)
    pass_on(1)
    w_b.next(2)
    pass_on_again(0)
    w_a[1].next(1)
    pass_on(3)
    pass_on_again(1)
    partial_sums(0)
    b_send(0)
    pass_on(2)
    partial_sums(1)
    a_send(0, 1)
    pass_on_again(3)
    w_a[0].next(2)
    a_send(0, 2)
    pass_on_again(2)
    partial_sums(3)
    a_send(1, 1)
    partial_sums(2)
    a_send(0, 3)
    b_send(1)
    a_send(1, 2)
    a_send(0, 4)
    a_send(1, 3)
    b_turn(0)
    a_send(1, 4)
    b_turn(1)
    w_b.next(3)
    a_turn(0)
    a_turn(1)
    w_a[0].next(3)
    b_end(0)
    b_end(1)
    w_b.next(4)
    a_end(1)
    a_end(0)
    squares()
    w_a[1].next(2)
    squares_x()
    w_a[0].next(4)
    w_a[1].next(3)
    squares_y()
    adam()
    swap_rows()
    w_a[1].next(4)
    n_c[0].start()
    n_b[0].start()
    d_hidden(1)
    n_c[1].start()
    n_b[0].next(1)
    swapped_rows()
    n_c[0].next(0)
    n_b[1].start()
    n_c[1].next(0)
    n_b[0].next(2)
    d_hidden(0)
    n_c[0].next(1)
    n_b[1].next(1)
    n_c[1].next(1)
    n_b[0].next(3)
    n_a.next(0)
    n_b[1].next(2)
    n_c[1].next(2)
    n_c[0].next(2)
    n_b[0].next(4)
    n_b[1].next(3)
    n_a.next(1)
    n_c[1].next(3)
    turn_back()
    gradients(0)
    n_c[0].next(3)
    n_a.next(2)
    n_b[1].next(4)
    gradients(1)
    n_c[0].next(4)
    gradients(2)
    n_c[1].next(4)
    gradients(3)
    n_a.next(3)
    gradients(4)
    gradients(5)
    gradients(6)
    gradients(7)
    n_a.next(4)
    for part in (*n_b, *n_c):
        part.finish()
    for copy in sent:
        copy.wait_send()
    assert count[0] == N_COPIES, (count[0], N_COPIES)


def store(*refs):
    sem = refs[-1]
    pairs = [(refs[5].at[i], refs[11].at[i]) for i in range(8)] + [(refs[i], refs[6 + i]) for i in range(5)]
    copies = [pltpu.make_async_copy(src, dst, sem.at[i]) for i, (src, dst) in enumerate(pairs)]
    for copy in copies:
        copy.start()
    for copy in copies:
        copy.wait()


def on_device(*args):
    vm = pltpu.VMEM
    shape = jax.ShapeDtypeStruct
    inside = pl.BlockSpec(memory_space=pltpu.VMEM)
    outside = pl.BlockSpec(memory_space=pltpu.HBM)
    wa = RS_A[0][1]
    shapes = (
        ((256, 1024), BF16), ((256, 1024), BF16), ((16, D), F32), ((16, D), F32), ((16, D), F32), ((8, 4, 32, D), BF16)
    )
    results = pl.pallas_call(
        kernel,
        out_shape=tuple(vm(*leaf) for leaf in shapes),
        in_specs=[outside] * 6,
        out_specs=(inside,) * 6,
        scratch_shapes=[
            vm((2, 256, D), BF16),
            vm((256, 1024), BF16),
            vm((256, 1024), BF16),
            vm((16, D), F32),
            vm((16, D), F32),
            vm((16, D), F32),
            vm((8, 4, 16, D), BF16),
            vm((2, 512, 256), BF16),
            vm((512, 256), BF16),
            vm((8, 4, 16, D), F32),
            vm((2, 2, 2, 16, wa), BF16),
            vm((2, 2, 2, 16, wa), BF16),
            vm((2, 2, 3, 4, 16, wa), BF16),
            vm((2, 2, 3, 4, 16, wa), BF16),
            vm((2, 3, 16, wa), BF16),
            vm((2, 3, 16, wa), BF16),
            vm((2, 4, 16, wa), F32),
            *(
                vm(leaf, kind)
                for _, wb in RS_B
                for leaf, kind in (
                    ((3, 8, 16, wb), BF16), ((3, 8, 16, wb), BF16), ((8, 16, wb), F32),
                    ((7, 16, wb), BF16), ((7, 16, wb), BF16),
                )
            ),
            vm((16, D), F32),
            vm((3, 8, 128), F32),
            vm((7, 8, 128), F32),
            vm((3, 8, 128), F32),
            vm((7, 8, 128), F32),
            vm((512, 256), F32),
            vm((512, 256), BF16),
            vm((512, 256), BF16),
            vm((2, 512, 256), F32),
            pltpu.SemaphoreType.DMA((N_COPIES,)),
            pltpu.SemaphoreType.DMA((N_COPIES,)),
            pltpu.SemaphoreType.DMA((6,)),
        ],
        compiler_params=pltpu.CompilerParams(
            collective_id=0, has_side_effects=True, vmem_limit_bytes=48 << 20
        ),
        name="step",
    )(*args)
    *rest, weight = pl.pallas_call(
        store,
        out_shape=tuple(shape(*leaf) for leaf in shapes),
        in_specs=[inside] * 6,
        out_specs=(outside,) * 6,
        scratch_shapes=[pltpu.SemaphoreType.DMA((13,))],
        compiler_params=pltpu.CompilerParams(vmem_limit_bytes=1 << 20),
        name="store",
    )(*(pltpu.with_memory_space_constraint(leaf, pltpu.VMEM) for leaf in results))
    return (*rest, weight.reshape(1024, D))


def solution(mesh):
    rows = P(("tensor", "dp"), None)
    both = P("dp", "tensor")
    return jax.shard_map(
        on_device,
        mesh=mesh,
        in_specs=(P("dp", None), both, both, rows, rows, rows),
        out_specs=(both, both, rows, rows, rows, P("tensor", None)),
        check_vma=False,
    )
```

```python
import functools

import jax
import jax.numpy as jnp
from jax import lax
from jax.experimental import pallas as pl
from jax.experimental.pallas import tpu as pltpu
from jax.sharding import PartitionSpec as P

D = 3072
FF = 4096
MESH = pl.DeviceIdType.MESH
F32 = jnp.float32
BF16 = jnp.bfloat16

RS_A = ((1024, 768), (2304, 768))
RS_B = ((0, 1024), (1792, 512))
CHUNKS = (RS_B[0], RS_A[0], RS_B[1], RS_A[1])
W_A = ((0, 768), (768, 640))
W_B = (1408, 1664)
N_C = ((0, 256), (256, 896))
N_A = (1152, 512)
N_B = (1664, 1408)
N_SWAP = (1152, 1920)

N_COPIES = (2 * 11 + 32) + 18 + 2 * (8 + 3) + 2 * (3 + 7) + 17 + 1 + 2 * 19 + 11 + 2 * 32


def kernel(
    d_in, g_in, u_in, ma_in, m1_in, m2_in,
    ggv, ugv, ma_o, m1_o, m2_o, ob,
    d2, gv, uv, mav, m1v, m2v, wg, ht, hr, gr,
    sah, rah, sa, ra, sax, rax, acca,
    sb0, rb0, accb0, sbz0, rbz0, sb1, rb1, accb1, sbz1, rbz1,
    g, sq, rz, rx, ry, dh, dhs, dhr, dht,
    ssem, rsem, lsem,
):
    dp, tensor = lax.axis_index("dp"), lax.axis_index("tensor")
    z, x, h = dp // 8, (dp // 2) % 4, dp % 2
    yl, c = tensor // 2, tensor % 2
    y = 2 * h + yl

    def device(zz, xx, yy, cc):
        return (zz * 8 + xx * 2 + yy // 2, (yy % 2) * 2 + cc)

    def at_z(k):
        return device((z + k + 8) % 8, x, y, c)

    def at_x(k):
        return device(z, (x + k + 4) % 4, y, c)

    sb, rb, accb, sbz, rbz = (sb0, sb1), (rb0, rb1), (accb0, accb1), (sbz0, sbz1), (rbz0, rbz1)
    across = device(z, x, 3 - y, c)
    beside = device(z, x, 2 * h + 1 - yl, c)
    mate = device(z, x, y, 1 - c)
    pair = (z * 8 + x * 2 + 1 - h, tensor)

    def near(k):
        i = (y * 2 + c + k) % 8
        return device(z, x, i // 2, i % 2)

    count = [0]
    sent = []

    def send(src, dst, to):
        i = count[0]
        count[0] += 1
        copy = pltpu.make_async_remote_copy(
            src_ref=src, dst_ref=dst, send_sem=ssem.at[i], recv_sem=rsem.at[i],
            device_id=to, device_id_type=MESH,
        )
        copy.start()
        sent.append(copy)
        return copy

    def load(src, dst, i):
        copy = pltpu.make_async_copy(src, dst, lsem.at[i])
        copy.start()
        return copy

    load_ma = load(ma_in, mav, 0)
    load_g = load(g_in, gv, 1)
    load_u = load(u_in, uv, 2)
    load_d = load(d_in, d2.at[0], 3)
    load_m1 = load(m1_in, m1v, 4)
    load_m2 = load(m2_in, m2v, 5)

    barrier = pltpu.get_barrier_semaphore()
    friends = (
        [at_z(k) for k in range(1, 8)]
        + [at_x(k) for k in range(1, 4)]
        + [near(k) for k in range(1, 8)]
    )
    for friend in friends:
        pl.semaphore_signal(barrier, inc=1, device_id=friend, device_id_type=MESH)
    load_ma.wait()
    wg[z, x] = mav[...].astype(BF16)
    pl.semaphore_wait(barrier, len(friends))

    class AlongXZ:
        def __init__(self, buf, rows, cols, to_pair=False):
            self.buf, self.rows, self.cols, self.to_pair = buf, rows, pl.ds(*cols), to_pair
            self.paired = []

        def start(self):
            own = self.buf.at[z, x, self.rows, self.cols]
            self.got = [send(own, own, at_x(k)) for k in (1, 3, 2)]

        def forward(self, block):
            if self.to_pair:
                self.paired.append(send(block, block, pair))

        def next(self, s):
            for copy in self.got:
                copy.wait_recv()
            a, b = (pl.ds(0, 4), pl.ds(0, 4)) if s < 3 else (pl.ds(0, 2), pl.ds(2, 2))
            if s < 4:
                up = self.buf.at[(z - s + 8) % 8, a, self.rows, self.cols]
                down = self.buf.at[(z + s) % 8, b, self.rows, self.cols]
                self.got = [send(up, up, at_z(1)), send(down, down, at_z(-1))]
            for k, part in ((-s, pl.ds(0, 4)), (s, pl.ds(0, 4)))[s == 0 :] if s < 4 else ((4, pl.ds(0, 4)),):
                self.forward(self.buf.at[(z + k + 8) % 8, part, self.rows, self.cols])

        def finish(self):
            for copy in self.paired:
                copy.wait_recv()

    class AlongZX:
        def __init__(self, buf, rows, cols):
            self.buf, self.rows, self.cols = buf, rows, cols
            self.spread = []

        def start(self):
            self.along_x(z)
            self.along_z(1)

        def along_x(self, zz):
            block = self.buf.at[zz, x, self.rows, pl.ds(*self.cols)]
            self.spread += [send(block, block, at_x(k)) for k in (1, 3, 2)]

        def along_z(self, s):
            c0, w = self.cols
            a, b = ((c0, w), (c0, w)) if s < 4 else ((c0, w // 2), (c0 + w // 2, w // 2))
            if s == 4 and w % 256:
                a, b = (c0, w // 2 - 64), (c0 + w // 2 - 64, w // 2 + 64)
            up = self.buf.at[(z - s + 9) % 8, x, self.rows, pl.ds(*a)]
            down = self.buf.at[(z + s - 1) % 8, x, self.rows, pl.ds(*b)]
            self.got = [send(up, up, at_z(1)), send(down, down, at_z(-1))]

        def next(self, s):
            for copy in self.got:
                copy.wait_recv()
            if s < 4:
                self.along_z(s + 1)
                self.along_x((z - s + 8) % 8)
                self.along_x((z + s) % 8)
            else:
                self.along_x((z + 4) % 8)

        def finish(self):
            for copy in self.spread:
                copy.wait_recv()

    everything = pl.ds(0, 16)
    w_a = [AlongXZ(wg, everything, cols) for cols in W_A]
    w_b = AlongZX(wg, everything, W_B)
    theirs = pl.ds(pl.multiple_of((1 - yl) * 128 + c * 64, 64), 64)
    mine = pl.ds(pl.multiple_of(yl * 128 + c * 64, 64), 64)
    cross, side, swap = [None] * 4, [None] * 4, [[] for _ in range(4)]

    def take(k):
        if k == 0:
            load_d.wait()
        cols = pl.ds(*CHUNKS[k])
        cross[k] = send(d2.at[0, theirs, cols], d2.at[1, theirs, cols], across)

    def pass_on(k):
        cross[k].wait_recv()
        block = d2.at[1, mine, pl.ds(*CHUNKS[k])]
        side[k] = send(block, block, beside)
        swap[k].append(send(block, block, mate))

    def pass_on_again(k):
        side[k].wait_recv()
        block = d2.at[1, theirs, pl.ds(*CHUNKS[k])]
        swap[k].append(send(block, block, mate))

    hid = []

    def hide():
        load_g.wait()
        load_u.wait()
        for i in range(8):
            cols = pl.ds(i * 128, 128)
            gate = gv[:, cols].astype(F32)
            hidden = gate * jax.nn.sigmoid(gate) * uv[:, cols].astype(F32)
            turned = hidden.astype(BF16).astype(F32).T.astype(BF16)
            for j in range(8):
                ht[j % 2, pl.ds((4 * i + j // 2) * 16, 16), :] = turned[j * 16 : j * 16 + 16, :]
        hid.append(send(ht.at[1 - h], hr, pair))

    def partial_sums(k):
        c0, w = CHUNKS[k]
        if k == 0:
            hid[0].wait_recv()
        for copy in swap[k]:
            copy.wait_recv()
        for i in range(w // 256):
            cols = pl.ds(c0 + i * 256, 256)
            acc = jnp.dot(ht[h], d2[0, :, cols], preferred_element_type=F32)
            acc += jnp.dot(hr[...], d2[1, :, cols], preferred_element_type=F32)
            gr[:, :, :, cols] = acc.reshape(8, 4, 16, 256)

    ring = [[[None, None] for _ in range(4)] for _ in RS_A]
    last_x = [None] * 2

    def a_send(j, s):
        cols = pl.ds(*RS_A[j])
        for way, sign in ((0, 1), (1, -1)):
            to = (z + sign * (5 - s) + 8) % 8
            if s == 1:
                part = pl.ds(2 * way, 2)
                sah[j, way] = gr[to, part, :, cols].astype(BF16)
                ring[j][0][way] = send(sah.at[j, way], rah.at[j, way], at_z(sign))
                continue
            ring[j][s - 2][way].wait_recv()
            if s == 2:
                part, rest = pl.ds(2 * way, 2), pl.ds(2 - 2 * way, 2)
                sa[j, way, 0, part] = (gr[to, part, :, cols] + rah[j, way].astype(F32)).astype(BF16)
                sa[j, way, 0, rest] = gr[to, rest, :, cols].astype(BF16)
            else:
                sa[j, way, s - 2] = (gr[to, :, :, cols] + ra[j, way, s - 3].astype(F32)).astype(BF16)
            ring[j][s - 1][way] = send(sa.at[j, way, s - 2], ra.at[j, way, s - 2], at_z(sign))

    def a_turn(j):
        cols = pl.ds(*RS_A[j])
        for way in (0, 1):
            ring[j][3][way].wait_recv()
        acca[j] = gr[z, :, :, cols] + ra[j, 0, 2].astype(F32) + ra[j, 1, 2].astype(F32)
        last_x[j] = []
        for k in (1, 3, 2):
            sax[j, k - 1] = acca[j, (x + k) % 4].astype(BF16)
            last_x[j].append(send(sax.at[j, k - 1], rax.at[j, k - 1], at_x(k)))

    def a_end(j):
        for copy in last_x[j]:
            copy.wait_recv()
        total = acca[j, x]
        for k in range(3):
            total += rax[j, k].astype(F32)
        g[:, pl.ds(*RS_A[j])] = total

    first_x = [None] * 2
    last_z = [None] * 2

    def b_send(j):
        first_x[j] = []
        for k in (1, 3, 2):
            sb[j][k - 1] = gr[:, (x + k) % 4, :, pl.ds(*RS_B[j])].astype(BF16)
            first_x[j].append(send(sb[j].at[k - 1], rb[j].at[k - 1], at_x(k)))

    def b_turn(j):
        for copy in first_x[j]:
            copy.wait_recv()
        total = gr[:, x, :, pl.ds(*RS_B[j])]
        for k in range(3):
            total += rb[j][k].astype(F32)
        accb[j][...] = total
        last_z[j] = []
        for k in (4, 3, 5, 2, 6, 1, 7):
            sbz[j][k - 1] = accb[j][(z + k) % 8].astype(BF16)
            last_z[j].append(send(sbz[j].at[k - 1], rbz[j].at[k - 1], at_z(k)))

    def b_end(j):
        for copy in last_z[j]:
            copy.wait_recv()
        total = accb[j][z]
        for k in range(7):
            total += rbz[j][k].astype(F32)
        g[:, pl.ds(*RS_B[j])] = total

    rounds = []

    def exchange(i, dst, hops):
        rounds.append([send(sq.at[i], dst.at[k - 1], to(k)) for k, to in hops])

    def arrived(i, dst, n):
        for copy in rounds[i]:
            copy.wait_recv()
        total = sq[i]
        for k in range(n):
            total += dst[k]
        return total

    def squares():
        square = g[...] * g[...]
        square = square[:8] + square[8:]
        total = square[:, 0:128]
        for i in range(1, 24):
            total += square[:, i * 128 : i * 128 + 128]
        sq[0] = total
        exchange(0, rz, [(k, at_z) for k in (4, 3, 5, 2, 6, 1, 7)])

    def squares_x():
        sq[1] = arrived(0, rz, 7)
        exchange(1, rx, [(k, at_x) for k in (2, 1, 3)])

    def squares_y():
        sq[2] = arrived(1, rx, 3)
        exchange(2, ry, [(k, near) for k in (4, 3, 5, 2, 6, 1, 7)])

    back = []

    def d_hidden(j):
        if j == 1:
            w_b.finish()
        acc = None
        for i in range(6):
            cols = pl.ds(i * 512, 512)
            part = lax.dot_general(
                wg[:, :, :, cols].reshape(512, 512), d2[j, :, cols],
                (((1,), (1,)), ((), ())), preferred_element_type=F32,
            )
            acc = part if acc is None else acc + part
        if j == 0:
            dh[...] = acc
        else:
            dhs[...] = acc.astype(BF16)
            back.append(send(dhs, dhr, pair))

    own, other = (pl.ds(pl.multiple_of(i * 16, 16), 16) for i in (h, 1 - h))

    def adam():
        load_m1.wait()
        load_m2.wait()
        total = arrived(2, ry, 7)
        factor = 1.0 / jnp.sqrt(jnp.sum(total, keepdims=True) / (FF * D) + 1e-06)
        clipped = g[...] * factor
        first = 0.9 * m1v[...] + 0.1 * clipped
        second = 0.95 * m2v[...] + 0.05 * clipped * clipped
        master = mav[...]
        master = master - 0.003 * (first / (jnp.sqrt(second) + 1e-08) + 0.1 * master)
        ob[z, x, own, :] = master.astype(BF16)
        ma_o[...] = master
        m1_o[...] = first
        m2_o[...] = second

    n_c = [AlongXZ(ob, own, cols, to_pair=True) for cols in N_C]
    n_a = AlongXZ(ob, pl.ds(0, 32), N_A)
    n_b = [AlongZX(ob, rows, N_B) for rows in (own, other)]
    swapped = []

    def swap_rows():
        block = ob.at[z, x, own, pl.ds(*N_SWAP)]
        swapped.append(send(block, block, pair))

    def swapped_rows():
        swapped[0].wait_recv()
        n_a.start()

    def turn_back():
        back[0].wait_recv()
        dht[h] = dh[...]
        dht[1 - h] = dhr[...].astype(F32)

    def gradients(i):
        cols = pl.ds(i * 128, 128)
        rows = [dht[j % 2, pl.ds((4 * i + j // 2) * 16, 16), :] for j in range(8)]
        dhid = jnp.concatenate(rows, axis=0).T
        gate = gv[:, cols].astype(F32)
        sig = jax.nn.sigmoid(gate)
        ugv[:, cols] = (dhid * (gate * sig)).astype(BF16)
        ggv[:, cols] = (dhid * uv[:, cols].astype(F32) * sig * (1.0 + gate * (1.0 - sig))).astype(BF16)

    w_a[1].start()
    take(0)
    w_b.start()
    w_a[0].start()
    hide()
    w_a[0].next(0)
    w_a[1].next(0)
    take(1)
    pass_on(0)
    w_b.next(1)
    take(2)
    w_a[0].next(1)
    take(3)
    w_a[1].next(1)
    pass_on(1)
    pass_on_again(0)
    w_b.next(2)
    partial_sums(0)
    pass_on(3)
    w_a[0].next(2)
    b_send(0)
    pass_on_again(1)
    pass_on_again(3)
    partial_sums(1)
    a_send(0, 1)
    w_b.next(3)
    partial_sums(3)
    a_send(1, 1)
    a_send(0, 2)
    pass_on(2)
    a_send(1, 2)
    pass_on_again(2)
    a_send(0, 3)
    a_send(1, 3)
    partial_sums(2)
    b_turn(0)
    a_send(0, 4)
    b_send(1)
    w_b.next(4)
    a_send(1, 4)
    b_turn(1)
    b_end(0)
    w_a[1].next(2)
    w_a[0].next(3)
    a_turn(0)
    a_turn(1)
    a_end(0)
    b_end(1)
    a_end(1)
    squares()
    squares_x()
    w_a[1].next(3)
    squares_y()
    adam()
    w_a[1].next(4)
    swap_rows()
    w_a[0].next(4)
    n_c[1].start()
    n_b[0].start()
    n_c[0].start()
    d_hidden(1)
    n_b[0].next(1)
    n_c[1].next(0)
    n_c[0].next(0)
    swapped_rows()
    n_b[1].start()
    d_hidden(0)
    n_c[1].next(1)
    n_b[0].next(2)
    n_b[1].next(1)
    n_c[0].next(1)
    n_a.next(0)
    n_c[1].next(2)
    n_b[1].next(2)
    n_c[0].next(2)
    n_b[0].next(3)
    n_a.next(1)
    n_c[1].next(3)
    turn_back()
    n_b[1].next(3)
    n_a.next(2)
    gradients(0)
    n_c[1].next(4)
    gradients(1)
    n_c[0].next(3)
    n_b[1].next(4)
    gradients(2)
    n_b[0].next(4)
    n_a.next(3)
    gradients(3)
    gradients(4)
    n_c[0].next(4)
    gradients(5)
    gradients(6)
    n_a.next(4)
    gradients(7)
    for part in (*n_b, *n_c):
        part.finish()
    for copy in sent:
        copy.wait_send()
    assert count[0] == N_COPIES, (count[0], N_COPIES)


def store(*refs):
    sem = refs[-1]
    pairs = [(refs[5].at[i], refs[11].at[i]) for i in range(8)] + [(refs[i], refs[6 + i]) for i in range(5)]
    copies = [pltpu.make_async_copy(src, dst, sem.at[i]) for i, (src, dst) in enumerate(pairs)]
    for copy in copies:
        copy.start()
    for copy in copies:
        copy.wait()


def on_device(*args):
    vm = pltpu.VMEM
    shape = jax.ShapeDtypeStruct
    inside = pl.BlockSpec(memory_space=pltpu.VMEM)
    outside = pl.BlockSpec(memory_space=pltpu.HBM)
    wa = RS_A[0][1]
    shapes = (
        ((256, 1024), BF16), ((256, 1024), BF16), ((16, D), F32), ((16, D), F32), ((16, D), F32), ((8, 4, 32, D), BF16)
    )
    results = pl.pallas_call(
        kernel,
        out_shape=tuple(vm(*leaf) for leaf in shapes),
        in_specs=[outside] * 6,
        out_specs=(inside,) * 6,
        scratch_shapes=[
            vm((2, 256, D), BF16),
            vm((256, 1024), BF16),
            vm((256, 1024), BF16),
            vm((16, D), F32),
            vm((16, D), F32),
            vm((16, D), F32),
            vm((8, 4, 16, D), BF16),
            vm((2, 512, 256), BF16),
            vm((512, 256), BF16),
            vm((8, 4, 16, D), F32),
            vm((2, 2, 2, 16, wa), BF16),
            vm((2, 2, 2, 16, wa), BF16),
            vm((2, 2, 3, 4, 16, wa), BF16),
            vm((2, 2, 3, 4, 16, wa), BF16),
            vm((2, 3, 16, wa), BF16),
            vm((2, 3, 16, wa), BF16),
            vm((2, 4, 16, wa), F32),
            *(
                vm(leaf, kind)
                for _, wb in RS_B
                for leaf, kind in (
                    ((3, 8, 16, wb), BF16), ((3, 8, 16, wb), BF16), ((8, 16, wb), F32),
                    ((7, 16, wb), BF16), ((7, 16, wb), BF16),
                )
            ),
            vm((16, D), F32),
            vm((3, 8, 128), F32),
            vm((7, 8, 128), F32),
            vm((3, 8, 128), F32),
            vm((7, 8, 128), F32),
            vm((512, 256), F32),
            vm((512, 256), BF16),
            vm((512, 256), BF16),
            vm((2, 512, 256), F32),
            pltpu.SemaphoreType.DMA((N_COPIES,)),
            pltpu.SemaphoreType.DMA((N_COPIES,)),
            pltpu.SemaphoreType.DMA((6,)),
        ],
        compiler_params=pltpu.CompilerParams(
            collective_id=0, has_side_effects=True, vmem_limit_bytes=48 << 20
        ),
        name="step",
    )(*args)
    *rest, weight = pl.pallas_call(
        store,
        out_shape=tuple(shape(*leaf) for leaf in shapes),
        in_specs=[inside] * 6,
        out_specs=(outside,) * 6,
        scratch_shapes=[pltpu.SemaphoreType.DMA((13,))],
        compiler_params=pltpu.CompilerParams(vmem_limit_bytes=1 << 20),
        name="store",
    )(*(pltpu.with_memory_space_constraint(leaf, pltpu.VMEM) for leaf in results))
    return (*rest, weight.reshape(1024, D))


def solution(mesh):
    rows = P(("tensor", "dp"), None)
    both = P("dp", "tensor")
    return jax.shard_map(
        on_device,
        mesh=mesh,
        in_specs=(P("dp", None), both, both, rows, rows, rows),
        out_specs=(both, both, rows, rows, rows, P("tensor", None)),
        check_vma=False,
    )
```

```python
import functools

import jax
import jax.numpy as jnp
from jax import lax
from jax.experimental import pallas as pl
from jax.experimental.pallas import tpu as pltpu
from jax.sharding import PartitionSpec as P

D = 3072
FF = 4096
MESH = pl.DeviceIdType.MESH
F32 = jnp.float32
BF16 = jnp.bfloat16

RS_A = ((768, 768), (2304, 768))
RS_B = ((0, 768), (1536, 768))
CHUNKS = (RS_B[0], RS_A[0], RS_B[1], RS_A[1])
W_A = ((0, 128), (128, 128))
W_B = (256, 2816)
N_C = ((0, 384), (384, 640))
N_A = (1024, 384)
N_B = (1408, 1664)
N_SWAP = (1024, 2048)

N_COPIES = (2 * 11 + 40) + 18 + 2 * (8 + 3) + 2 * (4 + 7) + 17 + 1 + 2 * 19 + 11 + 2 * 40


def kernel(
    d_in, g_in, u_in, ma_in, m1_in, m2_in,
    ggv, ugv, ma_o, m1_o, m2_o, ob,
    d2, gv, uv, mav, m1v, m2v, wg, ht, hr, gr,
    sah, rah, sa, ra, sax, rax, acca,
    sb0, rb0, sc0, rc0, accb0, sbz0, rbz0, sb1, rb1, sc1, rc1, accb1, sbz1, rbz1,
    g, sq, rz, rx, ry, dh, dhs, dhr, dht,
    ssem, rsem, lsem,
):
    dp, tensor = lax.axis_index("dp"), lax.axis_index("tensor")
    z, x, h = dp // 8, (dp // 2) % 4, dp % 2
    yl, c = tensor // 2, tensor % 2
    y = 2 * h + yl

    def device(zz, xx, yy, cc):
        return (zz * 8 + xx * 2 + yy // 2, (yy % 2) * 2 + cc)

    def at_z(k):
        return device((z + k + 8) % 8, x, y, c)

    def at_x(k):
        return device(z, (x + k + 4) % 4, y, c)

    sb, rb, sc, rc = (sb0, sb1), (rb0, rb1), (sc0, sc1), (rc0, rc1)
    accb, sbz, rbz = (accb0, accb1), (sbz0, sbz1), (rbz0, rbz1)
    across = device(z, x, 3 - y, c)
    beside = device(z, x, 2 * h + 1 - yl, c)
    mate = device(z, x, y, 1 - c)
    pair = (z * 8 + x * 2 + 1 - h, tensor)

    def near(k):
        i = (y * 2 + c + k) % 8
        return device(z, x, i // 2, i % 2)

    count = [0]
    sent = []

    def send(src, dst, to):
        i = count[0]
        count[0] += 1
        copy = pltpu.make_async_remote_copy(
            src_ref=src, dst_ref=dst, send_sem=ssem.at[i], recv_sem=rsem.at[i],
            device_id=to, device_id_type=MESH,
        )
        copy.start()
        sent.append(copy)
        return copy

    def load(src, dst, i):
        copy = pltpu.make_async_copy(src, dst, lsem.at[i])
        copy.start()
        return copy

    load_ma = load(ma_in, mav, 0)
    load_g = load(g_in, gv, 1)
    load_u = load(u_in, uv, 2)
    load_d = load(d_in, d2.at[0], 3)
    load_m1 = load(m1_in, m1v, 4)
    load_m2 = load(m2_in, m2v, 5)

    barrier = pltpu.get_barrier_semaphore()
    friends = (
        [at_z(k) for k in range(1, 8)]
        + [at_x(k) for k in range(1, 4)]
        + [near(k) for k in range(1, 8)]
    )
    for friend in friends:
        pl.semaphore_signal(barrier, inc=1, device_id=friend, device_id_type=MESH)
    load_ma.wait()
    wg[z, x] = mav[...].astype(BF16)
    pl.semaphore_wait(barrier, len(friends))

    class AlongXZ:
        def __init__(self, buf, rows, cols, to_pair=False):
            self.buf, self.rows, self.cols, self.to_pair = buf, rows, pl.ds(*cols), to_pair
            self.paired = []

        def start(self):
            own = self.buf.at[z, x, self.rows, self.cols]
            self.got = [send(own, own, at_x(k)) for k in (1, 3, 2)]

        def forward(self, block):
            if self.to_pair:
                self.paired.append(send(block, block, pair))

        def next(self, s):
            for copy in self.got:
                copy.wait_recv()
            a, b = (pl.ds(0, 4), pl.ds(0, 4)) if s < 3 else (pl.ds(0, 2), pl.ds(2, 2))
            if s < 4:
                up = self.buf.at[(z - s + 8) % 8, a, self.rows, self.cols]
                down = self.buf.at[(z + s) % 8, b, self.rows, self.cols]
                self.got = [send(up, up, at_z(1)), send(down, down, at_z(-1))]
            for k, part in ((-s, pl.ds(0, 4)), (s, pl.ds(0, 4)))[s == 0 :] if s < 4 else ((4, pl.ds(0, 4)),):
                self.forward(self.buf.at[(z + k + 8) % 8, part, self.rows, self.cols])

        def finish(self):
            for copy in self.paired:
                copy.wait_recv()

    class AlongZX:
        def __init__(self, buf, rows, cols):
            self.buf, self.rows, self.cols = buf, rows, cols
            self.spread, self.relayed = [], []

        def halves(self):
            c0, w = self.cols
            low = w // 256 * 128
            return pl.ds(c0, low), pl.ds(c0 + low, w - low)

        def start(self):
            self.along_x(z)
            self.along_z(1)

        def along_x(self, zz):
            block = self.buf.at[zz, x, self.rows, pl.ds(*self.cols)]
            self.spread.append((zz, send(block, block, at_x(1)), send(block, block, at_x(-1))))

        def relay(self, i):
            zz, below, above = self.spread[i]
            for copy, k, cols in zip((below, above), (1, -1), self.halves()):
                copy.wait_recv()
                block = self.buf.at[zz, (x - k + 4) % 4, self.rows, cols]
                self.relayed.append(send(block, block, at_x(k)))

        def along_z(self, s):
            a, b = (pl.ds(*self.cols),) * 2 if s < 4 else self.halves()
            up = self.buf.at[(z - s + 9) % 8, x, self.rows, a]
            down = self.buf.at[(z + s - 1) % 8, x, self.rows, b]
            self.got = [send(up, up, at_z(1)), send(down, down, at_z(-1))]

        def next(self, s):
            for copy in self.got:
                copy.wait_recv()
            if s < 4:
                self.along_z(s + 1)
                self.along_x((z - s + 8) % 8)
                self.along_x((z + s) % 8)
            else:
                self.along_x((z + 4) % 8)

        def finish(self):
            for copy in self.relayed:
                copy.wait_recv()

    everything = pl.ds(0, 16)
    w_a = [AlongXZ(wg, everything, cols) for cols in W_A]
    w_b = AlongZX(wg, everything, W_B)
    theirs = pl.ds(pl.multiple_of((1 - yl) * 128 + c * 64, 64), 64)
    mine = pl.ds(pl.multiple_of(yl * 128 + c * 64, 64), 64)
    cross, side, swap = [None] * 4, [None] * 4, [[] for _ in range(4)]

    def take(k):
        if k == 0:
            load_d.wait()
        cols = pl.ds(*CHUNKS[k])
        cross[k] = send(d2.at[0, theirs, cols], d2.at[1, theirs, cols], across)

    def pass_on(k):
        cross[k].wait_recv()
        block = d2.at[1, mine, pl.ds(*CHUNKS[k])]
        side[k] = send(block, block, beside)
        swap[k].append(send(block, block, mate))

    def pass_on_again(k):
        side[k].wait_recv()
        block = d2.at[1, theirs, pl.ds(*CHUNKS[k])]
        swap[k].append(send(block, block, mate))

    hid = []

    def hide():
        load_g.wait()
        load_u.wait()
        for i in range(8):
            cols = pl.ds(i * 128, 128)
            gate = gv[:, cols].astype(F32)
            hidden = gate * jax.nn.sigmoid(gate) * uv[:, cols].astype(F32)
            turned = hidden.astype(BF16).astype(F32).T.astype(BF16)
            for j in range(8):
                ht[j % 2, pl.ds((4 * i + j // 2) * 16, 16), :] = turned[j * 16 : j * 16 + 16, :]
        hid.append(send(ht.at[1 - h], hr, pair))

    def partial_sums(k):
        c0, w = CHUNKS[k]
        if k == 0:
            hid[0].wait_recv()
        for copy in swap[k]:
            copy.wait_recv()
        for i in range(w // 256):
            cols = pl.ds(c0 + i * 256, 256)
            acc = jnp.dot(ht[h], d2[0, :, cols], preferred_element_type=F32)
            acc += jnp.dot(hr[...], d2[1, :, cols], preferred_element_type=F32)
            gr[:, :, :, cols] = acc.reshape(8, 4, 16, 256)

    ring = [[[None, None] for _ in range(4)] for _ in RS_A]
    last_x = [None] * 2

    def a_send(j, s):
        cols = pl.ds(*RS_A[j])
        for way, sign in ((0, 1), (1, -1)):
            to = (z + sign * (5 - s) + 8) % 8
            if s == 1:
                part = pl.ds(2 * way, 2)
                sah[j, way] = gr[to, part, :, cols].astype(BF16)
                ring[j][0][way] = send(sah.at[j, way], rah.at[j, way], at_z(sign))
                continue
            ring[j][s - 2][way].wait_recv()
            if s == 2:
                part, rest = pl.ds(2 * way, 2), pl.ds(2 - 2 * way, 2)
                sa[j, way, 0, part] = (gr[to, part, :, cols] + rah[j, way].astype(F32)).astype(BF16)
                sa[j, way, 0, rest] = gr[to, rest, :, cols].astype(BF16)
            else:
                sa[j, way, s - 2] = (gr[to, :, :, cols] + ra[j, way, s - 3].astype(F32)).astype(BF16)
            ring[j][s - 1][way] = send(sa.at[j, way, s - 2], ra.at[j, way, s - 2], at_z(sign))

    def a_turn(j):
        cols = pl.ds(*RS_A[j])
        for way in (0, 1):
            ring[j][3][way].wait_recv()
        acca[j] = gr[z, :, :, cols] + ra[j, 0, 2].astype(F32) + ra[j, 1, 2].astype(F32)
        last_x[j] = []
        for k in (1, 3, 2):
            sax[j, k - 1] = acca[j, (x + k) % 4].astype(BF16)
            last_x[j].append(send(sax.at[j, k - 1], rax.at[j, k - 1], at_x(k)))

    def a_end(j):
        for copy in last_x[j]:
            copy.wait_recv()
        total = acca[j, x]
        for k in range(3):
            total += rax[j, k].astype(F32)
        g[:, pl.ds(*RS_A[j])] = total

    first_x, second_x = [None] * 2, [None] * 2
    last_z = [None] * 2

    def b_send(j):
        cols = pl.ds(*RS_B[j])
        first_x[j] = []
        for way, k in ((0, 1), (1, -1)):
            sb[j][way] = gr[pl.ds(4 * way, 4), (x + 2) % 4, :, cols].astype(BF16)
            first_x[j].append(send(sb[j].at[way], rb[j].at[way], at_x(k)))

    def b_pass(j):
        cols = pl.ds(*RS_B[j])
        second_x[j] = []
        for way, k in ((0, 1), (1, -1)):
            first_x[j][way].wait_recv()
            to = (x + k + 4) % 4
            part, rest = pl.ds(4 * way, 4), pl.ds(4 - 4 * way, 4)
            sc[j][way, part] = (gr[part, to, :, cols] + rb[j][way].astype(F32)).astype(BF16)
            sc[j][way, rest] = gr[rest, to, :, cols].astype(BF16)
            second_x[j].append(send(sc[j].at[way], rc[j].at[way], at_x(k)))

    def b_turn(j):
        for copy in second_x[j]:
            copy.wait_recv()
        total = gr[:, x, :, pl.ds(*RS_B[j])]
        for way in range(2):
            total += rc[j][way].astype(F32)
        accb[j][...] = total
        last_z[j] = []
        for k in (4, 3, 5, 2, 6, 1, 7):
            sbz[j][k - 1] = accb[j][(z + k) % 8].astype(BF16)
            last_z[j].append(send(sbz[j].at[k - 1], rbz[j].at[k - 1], at_z(k)))

    def b_end(j):
        for copy in last_z[j]:
            copy.wait_recv()
        total = accb[j][z]
        for k in range(7):
            total += rbz[j][k].astype(F32)
        g[:, pl.ds(*RS_B[j])] = total

    rounds = []

    def exchange(i, dst, hops):
        rounds.append([send(sq.at[i], dst.at[k - 1], to(k)) for k, to in hops])

    def arrived(i, dst, n):
        for copy in rounds[i]:
            copy.wait_recv()
        total = sq[i]
        for k in range(n):
            total += dst[k]
        return total

    def squares():
        square = g[...] * g[...]
        square = square[:8] + square[8:]
        total = square[:, 0:128]
        for i in range(1, 24):
            total += square[:, i * 128 : i * 128 + 128]
        sq[0] = total
        exchange(0, rz, [(k, at_z) for k in (4, 3, 5, 2, 6, 1, 7)])

    def squares_x():
        sq[1] = arrived(0, rz, 7)
        exchange(1, rx, [(k, at_x) for k in (2, 1, 3)])

    def squares_y():
        sq[2] = arrived(1, rx, 3)
        exchange(2, ry, [(k, near) for k in (4, 3, 5, 2, 6, 1, 7)])

    back = []

    def d_hidden(j):
        if j == 1:
            w_b.finish()
        acc = None
        for i in range(6):
            cols = pl.ds(i * 512, 512)
            part = lax.dot_general(
                wg[:, :, :, cols].reshape(512, 512), d2[j, :, cols],
                (((1,), (1,)), ((), ())), preferred_element_type=F32,
            )
            acc = part if acc is None else acc + part
        if j == 0:
            dh[...] = acc
        else:
            dhs[...] = acc.astype(BF16)
            back.append(send(dhs, dhr, pair))

    own, other = (pl.ds(pl.multiple_of(i * 16, 16), 16) for i in (h, 1 - h))

    def adam():
        load_m1.wait()
        load_m2.wait()
        total = arrived(2, ry, 7)
        factor = 1.0 / jnp.sqrt(jnp.sum(total, keepdims=True) / (FF * D) + 1e-06)
        clipped = g[...] * factor
        first = 0.9 * m1v[...] + 0.1 * clipped
        second = 0.95 * m2v[...] + 0.05 * clipped * clipped
        master = mav[...]
        master = master - 0.003 * (first / (jnp.sqrt(second) + 1e-08) + 0.1 * master)
        ob[z, x, own, :] = master.astype(BF16)
        ma_o[...] = master
        m1_o[...] = first
        m2_o[...] = second

    n_c = [AlongXZ(ob, own, cols, to_pair=True) for cols in N_C]
    n_a = AlongXZ(ob, pl.ds(0, 32), N_A)
    n_b = [AlongZX(ob, rows, N_B) for rows in (own, other)]
    swapped = []

    def swap_rows():
        block = ob.at[z, x, own, pl.ds(*N_SWAP)]
        swapped.append(send(block, block, pair))

    def swapped_rows():
        swapped[0].wait_recv()
        n_a.start()

    def turn_back():
        back[0].wait_recv()
        dht[h] = dh[...]
        dht[1 - h] = dhr[...].astype(F32)

    def gradients(i):
        cols = pl.ds(i * 128, 128)
        rows = [dht[j % 2, pl.ds((4 * i + j // 2) * 16, 16), :] for j in range(8)]
        dhid = jnp.concatenate(rows, axis=0).T
        gate = gv[:, cols].astype(F32)
        sig = jax.nn.sigmoid(gate)
        ugv[:, cols] = (dhid * (gate * sig)).astype(BF16)
        ggv[:, cols] = (dhid * uv[:, cols].astype(F32) * sig * (1.0 + gate * (1.0 - sig))).astype(BF16)

    take(0)
    take(1)
    w_b.start()
    w_a[0].start()
    take(2)
    w_a[1].start()
    pass_on(0)
    hide()
    take(3)
    w_b.next(1)
    pass_on(1)
    w_b.next(2)
    w_b.relay(0)
    w_b.relay(3)
    pass_on(3)
    w_a[1].next(0)
    pass_on_again(0)
    pass_on_again(1)
    w_b.next(3)
    pass_on(2)
    partial_sums(0)
    b_send(0)
    partial_sums(1)
    pass_on_again(3)
    a_send(0, 1)
    partial_sums(3)
    a_send(1, 1)
    pass_on_again(2)
    w_a[0].next(0)
    a_send(0, 2)
    partial_sums(2)
    a_send(1, 2)
    w_a[0].next(1)
    a_send(0, 3)
    b_send(1)
    a_send(1, 3)
    b_pass(0)
    a_send(0, 4)
    b_pass(1)
    w_b.relay(4)
    a_send(1, 4)
    w_b.next(4)
    w_a[1].next(1)
    b_turn(0)
    b_turn(1)
    w_a[1].next(2)
    a_turn(0)
    a_turn(1)
    b_end(0)
    w_a[1].next(3)
    a_end(1)
    w_a[0].next(2)
    w_b.relay(2)
    b_end(1)
    w_b.relay(1)
    a_end(0)
    squares()
    w_b.relay(5)
    w_a[0].next(3)
    squares_x()
    squares_y()
    w_b.relay(7)
    w_a[1].next(4)
    adam()
    n_c[1].start()
    w_b.relay(6)
    n_b[0].start()
    swap_rows()
    n_c[0].start()
    n_c[1].next(0)
    w_a[0].next(4)
    n_b[0].next(1)
    swapped_rows()
    d_hidden(1)
    n_b[1].start()
    n_b[0].relay(0)
    n_c[1].next(1)
    n_b[0].next(2)
    n_c[0].next(0)
    n_b[1].next(1)
    n_a.next(0)
    n_c[0].next(1)
    n_b[0].next(3)
    d_hidden(0)
    n_c[1].next(2)
    turn_back()
    n_b[1].next(2)
    n_b[0].relay(3)
    n_a.next(1)
    n_b[0].relay(1)
    n_b[1].relay(1)
    n_b[0].relay(4)
    n_b[0].relay(5)
    n_b[0].next(4)
    n_c[0].next(2)
    n_b[1].next(3)
    n_b[1].relay(2)
    n_b[1].relay(3)
    n_b[1].relay(0)
    n_c[1].next(3)
    n_a.next(2)
    n_b[0].relay(2)
    n_c[0].next(3)
    n_c[1].next(4)
    gradients(0)
    n_b[1].next(4)
    gradients(1)
    gradients(2)
    n_b[1].relay(6)
    n_a.next(3)
    n_b[0].relay(6)
    n_b[1].relay(5)
    gradients(3)
    n_b[0].relay(7)
    gradients(4)
    n_c[0].next(4)
    n_b[1].relay(7)
    gradients(5)
    n_b[1].relay(4)
    gradients(6)
    n_a.next(4)
    gradients(7)
    for part in (*n_b, *n_c):
        part.finish()
    for copy in sent:
        copy.wait_send()
    assert count[0] == N_COPIES, (count[0], N_COPIES)


def store(*refs):
    sem = refs[-1]
    pairs = [(refs[5].at[i], refs[11].at[i]) for i in range(8)] + [(refs[i], refs[6 + i]) for i in range(5)]
    copies = [pltpu.make_async_copy(src, dst, sem.at[i]) for i, (src, dst) in enumerate(pairs)]
    for copy in copies:
        copy.start()
    for copy in copies:
        copy.wait()


def on_device(*args):
    vm = pltpu.VMEM
    shape = jax.ShapeDtypeStruct
    inside = pl.BlockSpec(memory_space=pltpu.VMEM)
    outside = pl.BlockSpec(memory_space=pltpu.HBM)
    wa = RS_A[0][1]
    shapes = (
        ((256, 1024), BF16), ((256, 1024), BF16), ((16, D), F32), ((16, D), F32), ((16, D), F32), ((8, 4, 32, D), BF16)
    )
    results = pl.pallas_call(
        kernel,
        out_shape=tuple(vm(*leaf) for leaf in shapes),
        in_specs=[outside] * 6,
        out_specs=(inside,) * 6,
        scratch_shapes=[
            vm((2, 256, D), BF16),
            vm((256, 1024), BF16),
            vm((256, 1024), BF16),
            vm((16, D), F32),
            vm((16, D), F32),
            vm((16, D), F32),
            vm((8, 4, 16, D), BF16),
            vm((2, 512, 256), BF16),
            vm((512, 256), BF16),
            vm((8, 4, 16, D), F32),
            vm((2, 2, 2, 16, wa), BF16),
            vm((2, 2, 2, 16, wa), BF16),
            vm((2, 2, 3, 4, 16, wa), BF16),
            vm((2, 2, 3, 4, 16, wa), BF16),
            vm((2, 3, 16, wa), BF16),
            vm((2, 3, 16, wa), BF16),
            vm((2, 4, 16, wa), F32),
            *(
                vm(leaf, kind)
                for _, wb in RS_B
                for leaf, kind in (
                    ((2, 4, 16, wb), BF16), ((2, 4, 16, wb), BF16), ((2, 8, 16, wb), BF16), ((2, 8, 16, wb), BF16), ((8, 16, wb), F32),
                    ((7, 16, wb), BF16), ((7, 16, wb), BF16),
                )
            ),
            vm((16, D), F32),
            vm((3, 8, 128), F32),
            vm((7, 8, 128), F32),
            vm((3, 8, 128), F32),
            vm((7, 8, 128), F32),
            vm((512, 256), F32),
            vm((512, 256), BF16),
            vm((512, 256), BF16),
            vm((2, 512, 256), F32),
            pltpu.SemaphoreType.DMA((N_COPIES,)),
            pltpu.SemaphoreType.DMA((N_COPIES,)),
            pltpu.SemaphoreType.DMA((6,)),
        ],
        compiler_params=pltpu.CompilerParams(
            collective_id=0, has_side_effects=True, vmem_limit_bytes=48 << 20
        ),
        name="step",
    )(*args)
    *rest, weight = pl.pallas_call(
        store,
        out_shape=tuple(shape(*leaf) for leaf in shapes),
        in_specs=[inside] * 6,
        out_specs=(outside,) * 6,
        scratch_shapes=[pltpu.SemaphoreType.DMA((13,))],
        compiler_params=pltpu.CompilerParams(vmem_limit_bytes=1 << 20),
        name="store",
    )(*(pltpu.with_memory_space_constraint(leaf, pltpu.VMEM) for leaf in results))
    return (*rest, weight.reshape(1024, D))


def solution(mesh):
    rows = P(("tensor", "dp"), None)
    both = P("dp", "tensor")
    return jax.shard_map(
        on_device,
        mesh=mesh,
        in_specs=(P("dp", None), both, both, rows, rows, rows),
        out_specs=(both, both, rows, rows, rows, P("tensor", None)),
        check_vma=False,
    )
```

```python
import functools

import jax
import jax.numpy as jnp
from jax import lax
from jax.experimental import pallas as pl
from jax.experimental.pallas import tpu as pltpu
from jax.sharding import PartitionSpec as P

D = 3072
FF = 4096
MESH = pl.DeviceIdType.MESH
F32 = jnp.float32
BF16 = jnp.bfloat16

RS_A = ((768, 768), (2304, 768))
RS_B = ((0, 768), (1536, 768))
CHUNKS = (RS_B[0], RS_A[0], RS_B[1], RS_A[1])
W_A = ((0, 128), (128, 384))
W_B = (512, 2560)
N_C = ((0, 256), (256, 768))
N_A = (1024, 384)
N_B = (1408, 1664)
N_SWAP = (1024, 2048)

N_COPIES = (2 * 11 + 40) + 18 + 2 * (8 + 3) + 2 * (4 + 7) + 17 + 1 + 2 * 19 + 11 + 2 * 40


def kernel(
    d_in, g_in, u_in, ma_in, m1_in, m2_in,
    ggv, ugv, ma_o, m1_o, m2_o, ob,
    d2, gv, uv, mav, m1v, m2v, wg, ht, hr, gr,
    sah, rah, sa, ra, sax, rax, acca,
    sb0, rb0, sc0, rc0, accb0, sbz0, rbz0, sb1, rb1, sc1, rc1, accb1, sbz1, rbz1,
    g, sq, rz, rx, ry, dh, dhs, dhr, dht,
    ssem, rsem, lsem,
):
    dp, tensor = lax.axis_index("dp"), lax.axis_index("tensor")
    z, x, h = dp // 8, (dp // 2) % 4, dp % 2
    yl, c = tensor // 2, tensor % 2
    y = 2 * h + yl

    def device(zz, xx, yy, cc):
        return (zz * 8 + xx * 2 + yy // 2, (yy % 2) * 2 + cc)

    def at_z(k):
        return device((z + k + 8) % 8, x, y, c)

    def at_x(k):
        return device(z, (x + k + 4) % 4, y, c)

    sb, rb, sc, rc = (sb0, sb1), (rb0, rb1), (sc0, sc1), (rc0, rc1)
    accb, sbz, rbz = (accb0, accb1), (sbz0, sbz1), (rbz0, rbz1)
    across = device(z, x, 3 - y, c)
    beside = device(z, x, 2 * h + 1 - yl, c)
    mate = device(z, x, y, 1 - c)
    pair = (z * 8 + x * 2 + 1 - h, tensor)

    def near(k):
        i = (y * 2 + c + k) % 8
        return device(z, x, i // 2, i % 2)

    count = [0]
    sent = []

    def send(src, dst, to):
        i = count[0]
        count[0] += 1
        copy = pltpu.make_async_remote_copy(
            src_ref=src, dst_ref=dst, send_sem=ssem.at[i], recv_sem=rsem.at[i],
            device_id=to, device_id_type=MESH,
        )
        copy.start()
        sent.append(copy)
        return copy

    def load(src, dst, i):
        copy = pltpu.make_async_copy(src, dst, lsem.at[i])
        copy.start()
        return copy

    load_ma = load(ma_in, mav, 0)
    load_g = load(g_in, gv, 1)
    load_u = load(u_in, uv, 2)
    load_d = load(d_in, d2.at[0], 3)
    load_m1 = load(m1_in, m1v, 4)
    load_m2 = load(m2_in, m2v, 5)

    barrier = pltpu.get_barrier_semaphore()
    friends = (
        [at_z(k) for k in range(1, 8)]
        + [at_x(k) for k in range(1, 4)]
        + [near(k) for k in range(1, 8)]
    )
    for friend in friends:
        pl.semaphore_signal(barrier, inc=1, device_id=friend, device_id_type=MESH)
    load_ma.wait()
    wg[z, x] = mav[...].astype(BF16)
    pl.semaphore_wait(barrier, len(friends))

    class AlongXZ:
        def __init__(self, buf, rows, cols, to_pair=False):
            self.buf, self.rows, self.cols, self.to_pair = buf, rows, pl.ds(*cols), to_pair
            self.paired = []

        def start(self):
            own = self.buf.at[z, x, self.rows, self.cols]
            self.got = [send(own, own, at_x(k)) for k in (1, 3, 2)]

        def forward(self, block):
            if self.to_pair:
                self.paired.append(send(block, block, pair))

        def next(self, s):
            for copy in self.got:
                copy.wait_recv()
            a, b = (pl.ds(0, 4), pl.ds(0, 4)) if s < 3 else (pl.ds(0, 2), pl.ds(2, 2))
            if s < 4:
                up = self.buf.at[(z - s + 8) % 8, a, self.rows, self.cols]
                down = self.buf.at[(z + s) % 8, b, self.rows, self.cols]
                self.got = [send(up, up, at_z(1)), send(down, down, at_z(-1))]
            for k, part in ((-s, pl.ds(0, 4)), (s, pl.ds(0, 4)))[s == 0 :] if s < 4 else ((4, pl.ds(0, 4)),):
                self.forward(self.buf.at[(z + k + 8) % 8, part, self.rows, self.cols])

        def finish(self):
            for copy in self.paired:
                copy.wait_recv()

    class AlongZX:
        def __init__(self, buf, rows, cols):
            self.buf, self.rows, self.cols = buf, rows, cols
            self.spread, self.relayed = [], []

        def halves(self):
            c0, w = self.cols
            low = w // 256 * 128
            return pl.ds(c0, low), pl.ds(c0 + low, w - low)

        def start(self):
            self.along_x(z)
            self.along_z(1)

        def along_x(self, zz):
            block = self.buf.at[zz, x, self.rows, pl.ds(*self.cols)]
            self.spread.append((zz, send(block, block, at_x(1)), send(block, block, at_x(-1))))

        def relay(self, i):
            zz, below, above = self.spread[i]
            for copy, k, cols in zip((below, above), (1, -1), self.halves()):
                copy.wait_recv()
                block = self.buf.at[zz, (x - k + 4) % 4, self.rows, cols]
                self.relayed.append(send(block, block, at_x(k)))

        def along_z(self, s):
            a, b = (pl.ds(*self.cols),) * 2 if s < 4 else self.halves()
            up = self.buf.at[(z - s + 9) % 8, x, self.rows, a]
            down = self.buf.at[(z + s - 1) % 8, x, self.rows, b]
            self.got = [send(up, up, at_z(1)), send(down, down, at_z(-1))]

        def next(self, s):
            for copy in self.got:
                copy.wait_recv()
            if s < 4:
                self.along_z(s + 1)
                self.along_x((z - s + 8) % 8)
                self.along_x((z + s) % 8)
            else:
                self.along_x((z + 4) % 8)

        def finish(self):
            for copy in self.relayed:
                copy.wait_recv()

    everything = pl.ds(0, 16)
    w_a = [AlongXZ(wg, everything, cols) for cols in W_A]
    w_b = AlongZX(wg, everything, W_B)
    theirs = pl.ds(pl.multiple_of((1 - yl) * 128 + c * 64, 64), 64)
    mine = pl.ds(pl.multiple_of(yl * 128 + c * 64, 64), 64)
    cross, side, swap = [None] * 4, [None] * 4, [[] for _ in range(4)]

    def take(k):
        if k == 0:
            load_d.wait()
        cols = pl.ds(*CHUNKS[k])
        cross[k] = send(d2.at[0, theirs, cols], d2.at[1, theirs, cols], across)

    def pass_on(k):
        cross[k].wait_recv()
        block = d2.at[1, mine, pl.ds(*CHUNKS[k])]
        side[k] = send(block, block, beside)
        swap[k].append(send(block, block, mate))

    def pass_on_again(k):
        side[k].wait_recv()
        block = d2.at[1, theirs, pl.ds(*CHUNKS[k])]
        swap[k].append(send(block, block, mate))

    hid = []

    def hide():
        load_g.wait()
        load_u.wait()
        for i in range(8):
            cols = pl.ds(i * 128, 128)
            gate = gv[:, cols].astype(F32)
            hidden = gate * jax.nn.sigmoid(gate) * uv[:, cols].astype(F32)
            turned = hidden.astype(BF16).astype(F32).T.astype(BF16)
            for j in range(8):
                ht[j % 2, pl.ds((4 * i + j // 2) * 16, 16), :] = turned[j * 16 : j * 16 + 16, :]
        hid.append(send(ht.at[1 - h], hr, pair))

    def partial_sums(k):
        c0, w = CHUNKS[k]
        if k == 0:
            hid[0].wait_recv()
        for copy in swap[k]:
            copy.wait_recv()
        for i in range(w // 256):
            cols = pl.ds(c0 + i * 256, 256)
            acc = jnp.dot(ht[h], d2[0, :, cols], preferred_element_type=F32)
            acc += jnp.dot(hr[...], d2[1, :, cols], preferred_element_type=F32)
            gr[:, :, :, cols] = acc.reshape(8, 4, 16, 256)

    ring = [[[None, None] for _ in range(4)] for _ in RS_A]
    last_x = [None] * 2

    def a_send(j, s):
        cols = pl.ds(*RS_A[j])
        for way, sign in ((0, 1), (1, -1)):
            to = (z + sign * (5 - s) + 8) % 8
            if s == 1:
                part = pl.ds(2 * way, 2)
                sah[j, way] = gr[to, part, :, cols].astype(BF16)
                ring[j][0][way] = send(sah.at[j, way], rah.at[j, way], at_z(sign))
                continue
            ring[j][s - 2][way].wait_recv()
            if s == 2:
                part, rest = pl.ds(2 * way, 2), pl.ds(2 - 2 * way, 2)
                sa[j, way, 0, part] = (gr[to, part, :, cols] + rah[j, way].astype(F32)).astype(BF16)
                sa[j, way, 0, rest] = gr[to, rest, :, cols].astype(BF16)
            else:
                sa[j, way, s - 2] = (gr[to, :, :, cols] + ra[j, way, s - 3].astype(F32)).astype(BF16)
            ring[j][s - 1][way] = send(sa.at[j, way, s - 2], ra.at[j, way, s - 2], at_z(sign))

    def a_turn(j):
        cols = pl.ds(*RS_A[j])
        for way in (0, 1):
            ring[j][3][way].wait_recv()
        acca[j] = gr[z, :, :, cols] + ra[j, 0, 2].astype(F32) + ra[j, 1, 2].astype(F32)
        last_x[j] = []
        for k in (1, 3, 2):
            sax[j, k - 1] = acca[j, (x + k) % 4].astype(BF16)
            last_x[j].append(send(sax.at[j, k - 1], rax.at[j, k - 1], at_x(k)))

    def a_end(j):
        for copy in last_x[j]:
            copy.wait_recv()
        total = acca[j, x]
        for k in range(3):
            total += rax[j, k].astype(F32)
        g[:, pl.ds(*RS_A[j])] = total

    first_x, second_x = [None] * 2, [None] * 2
    last_z = [None] * 2

    def b_send(j):
        cols = pl.ds(*RS_B[j])
        first_x[j] = []
        for way, k in ((0, 1), (1, -1)):
            sb[j][way] = gr[pl.ds(4 * way, 4), (x + 2) % 4, :, cols].astype(BF16)
            first_x[j].append(send(sb[j].at[way], rb[j].at[way], at_x(k)))

    def b_pass(j):
        cols = pl.ds(*RS_B[j])
        second_x[j] = []
        for way, k in ((0, 1), (1, -1)):
            first_x[j][way].wait_recv()
            to = (x + k + 4) % 4
            part, rest = pl.ds(4 * way, 4), pl.ds(4 - 4 * way, 4)
            sc[j][way, part] = (gr[part, to, :, cols] + rb[j][way].astype(F32)).astype(BF16)
            sc[j][way, rest] = gr[rest, to, :, cols].astype(BF16)
            second_x[j].append(send(sc[j].at[way], rc[j].at[way], at_x(k)))

    def b_turn(j):
        for copy in second_x[j]:
            copy.wait_recv()
        total = gr[:, x, :, pl.ds(*RS_B[j])]
        for way in range(2):
            total += rc[j][way].astype(F32)
        accb[j][...] = total
        last_z[j] = []
        for k in (4, 3, 5, 2, 6, 1, 7):
            sbz[j][k - 1] = accb[j][(z + k) % 8].astype(BF16)
            last_z[j].append(send(sbz[j].at[k - 1], rbz[j].at[k - 1], at_z(k)))

    def b_end(j):
        for copy in last_z[j]:
            copy.wait_recv()
        total = accb[j][z]
        for k in range(7):
            total += rbz[j][k].astype(F32)
        g[:, pl.ds(*RS_B[j])] = total

    rounds = []

    def exchange(i, dst, hops):
        rounds.append([send(sq.at[i], dst.at[k - 1], to(k)) for k, to in hops])

    def arrived(i, dst, n):
        for copy in rounds[i]:
            copy.wait_recv()
        total = sq[i]
        for k in range(n):
            total += dst[k]
        return total

    def squares():
        square = g[...] * g[...]
        square = square[:8] + square[8:]
        total = square[:, 0:128]
        for i in range(1, 24):
            total += square[:, i * 128 : i * 128 + 128]
        sq[0] = total
        exchange(0, rz, [(k, at_z) for k in (4, 3, 5, 2, 6, 1, 7)])

    def squares_x():
        sq[1] = arrived(0, rz, 7)
        exchange(1, rx, [(k, at_x) for k in (2, 1, 3)])

    def squares_y():
        sq[2] = arrived(1, rx, 3)
        exchange(2, ry, [(k, near) for k in (4, 3, 5, 2, 6, 1, 7)])

    back = []

    def d_hidden(j):
        if j == 1:
            w_b.finish()
        acc = None
        for i in range(6):
            cols = pl.ds(i * 512, 512)
            part = lax.dot_general(
                wg[:, :, :, cols].reshape(512, 512), d2[j, :, cols],
                (((1,), (1,)), ((), ())), preferred_element_type=F32,
            )
            acc = part if acc is None else acc + part
        if j == 0:
            dh[...] = acc
        else:
            dhs[...] = acc.astype(BF16)
            back.append(send(dhs, dhr, pair))

    own, other = (pl.ds(pl.multiple_of(i * 16, 16), 16) for i in (h, 1 - h))

    def adam():
        load_m1.wait()
        load_m2.wait()
        total = arrived(2, ry, 7)
        factor = 1.0 / jnp.sqrt(jnp.sum(total, keepdims=True) / (FF * D) + 1e-06)
        clipped = g[...] * factor
        first = 0.9 * m1v[...] + 0.1 * clipped
        second = 0.95 * m2v[...] + 0.05 * clipped * clipped
        master = mav[...]
        master = master - 0.003 * (first / (jnp.sqrt(second) + 1e-08) + 0.1 * master)
        ob[z, x, own, :] = master.astype(BF16)
        ma_o[...] = master
        m1_o[...] = first
        m2_o[...] = second

    n_c = [AlongXZ(ob, own, cols, to_pair=True) for cols in N_C]
    n_a = AlongXZ(ob, pl.ds(0, 32), N_A)
    n_b = [AlongZX(ob, rows, N_B) for rows in (own, other)]
    swapped = []

    def swap_rows():
        block = ob.at[z, x, own, pl.ds(*N_SWAP)]
        swapped.append(send(block, block, pair))

    def swapped_rows():
        swapped[0].wait_recv()
        n_a.start()

    def turn_back():
        back[0].wait_recv()
        dht[h] = dh[...]
        dht[1 - h] = dhr[...].astype(F32)

    def gradients(i):
        cols = pl.ds(i * 128, 128)
        rows = [dht[j % 2, pl.ds((4 * i + j // 2) * 16, 16), :] for j in range(8)]
        dhid = jnp.concatenate(rows, axis=0).T
        gate = gv[:, cols].astype(F32)
        sig = jax.nn.sigmoid(gate)
        ugv[:, cols] = (dhid * (gate * sig)).astype(BF16)
        ggv[:, cols] = (dhid * uv[:, cols].astype(F32) * sig * (1.0 + gate * (1.0 - sig))).astype(BF16)

    take(0)
    take(1)
    take(2)
    w_a[0].start()
    w_a[1].start()
    w_b.start()
    pass_on(0)
    w_a[0].next(0)
    take(3)
    hide()
    w_b.next(1)
    pass_on(1)
    w_a[0].next(1)
    w_a[1].next(0)
    w_b.next(2)
    w_a[1].next(1)
    pass_on_again(1)
    pass_on(3)
    w_a[0].next(2)
    w_b.next(3)
    pass_on_again(0)
    partial_sums(0)
    partial_sums(1)
    pass_on_again(3)
    b_send(0)
    a_send(0, 1)
    pass_on(2)
    partial_sums(3)
    a_send(1, 1)
    a_send(0, 2)
    pass_on_again(2)
    w_b.relay(3)
    b_pass(0)
    a_send(1, 2)
    partial_sums(2)
    w_a[0].next(3)
    a_send(0, 3)
    b_send(1)
    a_send(1, 3)
    b_turn(0)
    w_a[0].next(4)
    a_send(0, 4)
    b_pass(1)
    w_b.relay(1)
    a_send(1, 4)
    w_b.relay(4)
    b_turn(1)
    w_b.relay(5)
    a_turn(1)
    w_b.relay(6)
    a_turn(0)
    w_a[1].next(2)
    w_b.relay(2)
    b_end(0)
    w_a[1].next(3)
    a_end(1)
    w_b.next(4)
    b_end(1)
    a_end(0)
    squares()
    w_b.relay(0)
    w_a[1].next(4)
    squares_x()
    squares_y()
    w_b.relay(7)
    adam()
    n_c[0].start()
    swap_rows()
    n_b[0].start()
    n_c[1].start()
    d_hidden(1)
    n_b[0].next(1)
    n_c[0].next(0)
    swapped_rows()
    n_c[1].next(0)
    n_b[1].start()
    n_b[0].next(2)
    n_c[0].next(1)
    d_hidden(0)
    n_b[0].relay(0)
    n_c[1].next(1)
    n_b[0].relay(1)
    n_b[1].next(1)
    turn_back()
    n_b[0].next(3)
    n_a.next(0)
    n_c[0].next(2)
    n_b[1].next(2)
    n_b[0].relay(3)
    n_c[1].next(2)
    n_b[1].relay(2)
    n_b[0].next(4)
    n_b[0].relay(4)
    n_b[1].relay(1)
    n_c[0].next(3)
    n_a.next(1)
    n_b[1].next(3)
    n_c[1].next(3)
    n_b[1].relay(4)
    n_b[1].relay(0)
    n_a.next(2)
    n_b[1].next(4)
    n_b[1].relay(6)
    n_b[0].relay(6)
    gradients(0)
    n_b[1].relay(5)
    n_b[0].relay(7)
    gradients(1)
    gradients(2)
    n_c[0].next(4)
    n_b[1].relay(7)
    gradients(3)
    n_c[1].next(4)
    gradients(4)
    n_a.next(3)
    n_b[0].relay(5)
    gradients(5)
    gradients(6)
    n_b[0].relay(2)
    n_b[1].relay(3)
    gradients(7)
    n_a.next(4)
    for part in (*n_b, *n_c):
        part.finish()
    for copy in sent:
        copy.wait_send()
    assert count[0] == N_COPIES, (count[0], N_COPIES)


def store(*refs):
    sem = refs[-1]
    pairs = [(refs[5].at[i], refs[11].at[i]) for i in range(8)] + [(refs[i], refs[6 + i]) for i in range(5)]
    copies = [pltpu.make_async_copy(src, dst, sem.at[i]) for i, (src, dst) in enumerate(pairs)]
    for copy in copies:
        copy.start()
    for copy in copies:
        copy.wait()


def on_device(*args):
    vm = pltpu.VMEM
    shape = jax.ShapeDtypeStruct
    inside = pl.BlockSpec(memory_space=pltpu.VMEM)
    outside = pl.BlockSpec(memory_space=pltpu.HBM)
    wa = RS_A[0][1]
    shapes = (
        ((256, 1024), BF16), ((256, 1024), BF16), ((16, D), F32), ((16, D), F32), ((16, D), F32), ((8, 4, 32, D), BF16)
    )
    results = pl.pallas_call(
        kernel,
        out_shape=tuple(vm(*leaf) for leaf in shapes),
        in_specs=[outside] * 6,
        out_specs=(inside,) * 6,
        scratch_shapes=[
            vm((2, 256, D), BF16),
            vm((256, 1024), BF16),
            vm((256, 1024), BF16),
            vm((16, D), F32),
            vm((16, D), F32),
            vm((16, D), F32),
            vm((8, 4, 16, D), BF16),
            vm((2, 512, 256), BF16),
            vm((512, 256), BF16),
            vm((8, 4, 16, D), F32),
            vm((2, 2, 2, 16, wa), BF16),
            vm((2, 2, 2, 16, wa), BF16),
            vm((2, 2, 3, 4, 16, wa), BF16),
            vm((2, 2, 3, 4, 16, wa), BF16),
            vm((2, 3, 16, wa), BF16),
            vm((2, 3, 16, wa), BF16),
            vm((2, 4, 16, wa), F32),
            *(
                vm(leaf, kind)
                for _, wb in RS_B
                for leaf, kind in (
                    ((2, 4, 16, wb), BF16), ((2, 4, 16, wb), BF16), ((2, 8, 16, wb), BF16), ((2, 8, 16, wb), BF16), ((8, 16, wb), F32),
                    ((7, 16, wb), BF16), ((7, 16, wb), BF16),
                )
            ),
            vm((16, D), F32),
            vm((3, 8, 128), F32),
            vm((7, 8, 128), F32),
            vm((3, 8, 128), F32),
            vm((7, 8, 128), F32),
            vm((512, 256), F32),
            vm((512, 256), BF16),
            vm((512, 256), BF16),
            vm((2, 512, 256), F32),
            pltpu.SemaphoreType.DMA((N_COPIES,)),
            pltpu.SemaphoreType.DMA((N_COPIES,)),
            pltpu.SemaphoreType.DMA((6,)),
        ],
        compiler_params=pltpu.CompilerParams(
            collective_id=0, has_side_effects=True, vmem_limit_bytes=48 << 20
        ),
        name="step",
    )(*args)
    *rest, weight = pl.pallas_call(
        store,
        out_shape=tuple(shape(*leaf) for leaf in shapes),
        in_specs=[inside] * 6,
        out_specs=(outside,) * 6,
        scratch_shapes=[pltpu.SemaphoreType.DMA((13,))],
        compiler_params=pltpu.CompilerParams(vmem_limit_bytes=1 << 20),
        name="store",
    )(*(pltpu.with_memory_space_constraint(leaf, pltpu.VMEM) for leaf in results))
    return (*rest, weight.reshape(1024, D))


def solution(mesh):
    rows = P(("tensor", "dp"), None)
    both = P("dp", "tensor")
    return jax.shard_map(
        on_device,
        mesh=mesh,
        in_specs=(P("dp", None), both, both, rows, rows, rows),
        out_specs=(both, both, rows, rows, rows, P("tensor", None)),
        check_vma=False,
    )
```
